512 devices in a mesh: section: 8 (over y_lo, core), dp: 64 (over z, x, y_hi).
Axes of the slice: x: 4, y: 8 (y_hi: 2, y_lo: 4; y = y_hi * 4 + y_lo), z: 8, core: 2. Of those that a mesh axis runs over, the one named last changes fastest.
Arguments:
- acts: float32 [8, 8192, 1024], P('section', 'dp'), may hold values from -6 to 6
- grads: float32 [8, 8192, 1024], P('section', 'dp'), may hold values from -0.6 to 0.6
- in_proj: bfloat16 [8, 2048, 512], P('section', 'dp'), may hold values from -0.25 to 0.25
- out_proj: bfloat16 [8, 2048, 512], P('section', 'dp'), may hold values from -0.125 to 0.125
- gain: float32 [8, 512], P('section'), may hold values from 0.1 to 1.9
Outputs:
- acts_out: float32 [8, 8192, 1024], P('section', 'dp')
- grads_out: float32 [8, 8192, 1024], P('section', 'dp')
- out_proj_grad: float32 [8, 2048, 512], P('section', 'dp')
The draws below stay inside these ranges and needn't reach their ends.
All inputs are finite; a program needn't handle non-finite values.
Results may differ from the reference program's by a relative error of at most 0.012.
Values may be sent and summed in bfloat16 or wider, within the bound.
No kernel may reach another device: no remote copies, remote signals or barrier semaphores. Data moves between devices by JAX's collectives and lax.ppermute only.
A program may use at most 64 MiB of HBM per device.

```python
import jax
import jax.numpy as jnp
from jax import lax

D = 1024
HALF = 512
FF_W = 2048
TOKENS = 8192
TICKS = 4
N_SECTION = 8


def levels(stream_key, shape, shards, low, high):
    def one(dim, parts):
        heights = jax.random.uniform(jax.random.fold_in(jax.random.fold_in(stream_key, 6), dim), (parts,), jnp.float32, low / len(shards), high / len(shards))
        return jnp.repeat(jnp.exp(heights), shape[dim] // parts).reshape((-1,) + (1,) * (len(shape) - dim - 1))

    factor_of = one(*shards[0])
    for cut in shards[1:]:
        factor_of = factor_of * one(*cut)
    return factor_of


def centred(rng, dims, width, limit, shards=(), dtype=jnp.bfloat16):
    drawn = width * jax.random.normal(rng, dims, jnp.float32)
    if shards:
        drawn = drawn * levels(rng, dims, shards, -0.22, 0.18)
    return jnp.clip(drawn, -limit, limit).astype(dtype)


def setup_inputs(seed: int = 0) -> dict:
    arg_keys = jax.random.split(jax.random.key(seed), 6)
    return {
        "acts": centred(arg_keys[0], (N_SECTION, TOKENS, D), 1.0, 6.0, ((0, 8), (1, 64)), jnp.float32),
        "grads": centred(arg_keys[1], (N_SECTION, TOKENS, D), 0.1, 0.6, ((0, 8), (1, 64)), jnp.float32),
        "in_proj": centred(arg_keys[2], (N_SECTION, FF_W, HALF), HALF ** -0.5, 0.25, ((0, 8), (1, 64))),
        "out_proj": centred(arg_keys[3], (N_SECTION, FF_W, HALF), FF_W ** -0.5, 0.125, ((0, 8), (1, 64))),
        "gain": jnp.clip(1.0 + 0.18 * jax.random.normal(arg_keys[4], (N_SECTION, HALF), jnp.float32), 0.1, 1.9),
    }


coupling_scale = 32.0 ** 0.25
rms_epsilon = 1e-06
root_half = 0.7071067811865476
inv_root_two_pi = 0.3989422804014327

def normalize(first_half, gain_row):
    inv_rms = lax.rsqrt(lax.optimization_barrier(jnp.mean(first_half * first_half, axis=-1, keepdims=True)) + rms_epsilon)
    normed = (first_half * inv_rms * gain_row).astype(jnp.bfloat16)
    return (inv_rms, normed)

def gelu_slope(preact):
    normal_cdf = 0.5 * (1.0 + lax.erf(preact * root_half))
    density = jnp.exp(-0.5 * preact * preact) * inv_root_two_pi
    return (preact * normal_cdf, normal_cdf + preact * density)

def half_block(normed, cotangent, weight_in, weight_out):
    preact = lax.dot_general(normed, weight_in, (((1,), (1,)), ((), ())), preferred_element_type=jnp.float32)
    hidden, slopes = gelu_slope(preact)
    hidden_b = hidden.astype(jnp.bfloat16)
    branch = jnp.dot(hidden_b, weight_out, preferred_element_type=jnp.float32)
    hidden_grad = lax.dot_general(cotangent, weight_out, (((1,), (1,)), ((), ())), preferred_element_type=jnp.float32)
    pre_grad = (hidden_grad * slopes).astype(jnp.bfloat16)
    norm_grad = jnp.dot(pre_grad, weight_in, preferred_element_type=jnp.float32)
    return (hidden_b, branch, norm_grad)

def invert_step(first_half, second_half, first_grad, second_grad, inv_rms, gain_row, branch, norm_grad):
    scaled = norm_grad * gain_row
    inner = lax.optimization_barrier(jnp.mean(first_half * scaled, axis=-1, keepdims=True))
    input_grad = inv_rms * scaled - first_half * (inv_rms * inv_rms * inv_rms) * inner
    new_acts = jnp.concatenate([(second_half - branch) / coupling_scale, first_half], axis=-1)
    new_grads = jnp.concatenate([coupling_scale * second_grad, first_grad + input_grad], axis=-1)
    return (new_acts, new_grads)

def section_tick(section_inputs):
    acts_s, grads_s, weight_in, weight_out, gain_row = section_inputs
    feature_half = acts_s.shape[1] // 2
    first_half = acts_s[:, :feature_half]
    second_half = acts_s[:, feature_half:]
    first_grad = grads_s[:, :feature_half]
    second_grad = grads_s[:, feature_half:]
    inv_rms, normed = normalize(first_half, gain_row)
    cotangent = second_grad.astype(jnp.bfloat16)
    hidden_b, branch, norm_grad = half_block(normed, cotangent, weight_in, weight_out)
    new_acts, new_grads = invert_step(first_half, second_half, first_grad, second_grad, inv_rms, gain_row, branch, norm_grad)
    contribution = lax.dot_general(hidden_b, cotangent, (((0,), (0,)), ((), ())), preferred_element_type=jnp.float32)
    return (new_acts, new_grads, contribution)

def reference(acts, grads, in_proj, out_proj, gain):
    held_acts = acts
    held_grads = grads
    grad_total = jnp.zeros((N_SECTION, FF_W, HALF), jnp.float32)
    for tick_index in range(TICKS):
        live_count = N_SECTION - tick_index
        new_acts, new_grads, contribution = lax.map(section_tick, (held_acts[:live_count], held_grads[:live_count], in_proj[:live_count], out_proj[:live_count], gain[:live_count]))
        grad_total = grad_total + jnp.concatenate([contribution, jnp.zeros((tick_index, FF_W, HALF), jnp.float32)], axis=0)
        zero_rows = jnp.zeros((tick_index + 1, TOKENS, D), jnp.float32)
        held_acts = jnp.concatenate([new_acts[1:], zero_rows], axis=0)
        held_grads = jnp.concatenate([new_grads[1:], zero_rows], axis=0)
    return (held_acts, held_grads, grad_total)
```

```python
import jax
import jax.numpy as jnp
from jax import lax
from jax.sharding import PartitionSpec as P

coupling_scale = 32.0**0.25
rms_epsilon = 1e-06
root_half = 0.7071067811865476
inv_root_two_pi = 0.3989422804014327

x_size = 4
pair_size = 2


def column_groups(dp_size):
    z_size = dp_size // (x_size * pair_size)
    at = lambda z, x, y: (z * x_size + x) * pair_size + y
    along_x = [[at(z, x, y) for x in range(x_size)] for z in range(z_size) for y in range(pair_size)]
    across_x = [[at(z, x, y) for z in range(z_size) for y in range(pair_size)] for x in range(x_size)]
    return along_x, across_x


def exchanged(blocks, groups):
    return lax.all_to_all(blocks, "dp", 0, 0, axis_index_groups=groups, tiled=True)


def copied_to_group(block, groups):
    size = len(groups[0])
    return exchanged(jnp.tile(block, (size, 1)), groups)


def passed_back(block):
    devices = range(lax.axis_size("section"))
    return lax.ppermute(block, "section", [(i, i - 1) for i in devices if i])


def forward(first, second, gain_row, weight_in, weight_out):
    inv_rms = lax.rsqrt(jnp.mean(first * first, axis=-1, keepdims=True) + rms_epsilon)
    normed = (first * inv_rms * gain_row).astype(jnp.bfloat16)
    preact = lax.dot_general(
        normed, weight_in, (((1,), (1,)), ((), ())), preferred_element_type=jnp.float32
    )
    normal_cdf = 0.5 * (1.0 + lax.erf(preact * root_half))
    density = jnp.exp(-0.5 * preact * preact) * inv_root_two_pi
    hidden = (preact * normal_cdf).astype(jnp.bfloat16)
    slopes = normal_cdf + preact * density
    branch = jnp.dot(hidden, weight_out, preferred_element_type=jnp.float32)
    return inv_rms, hidden, slopes, (second - branch) / coupling_scale


def backward(first, inv_rms, slopes, cotangent, first_grad, gain_row, weight_in, weight_out):
    hidden_grad = lax.dot_general(
        cotangent, weight_out, (((1,), (1,)), ((), ())), preferred_element_type=jnp.float32
    )
    pre_grad = (hidden_grad * slopes).astype(jnp.bfloat16)
    scaled = jnp.dot(pre_grad, weight_in, preferred_element_type=jnp.float32) * gain_row
    inner = jnp.mean(first * scaled, axis=-1, keepdims=True)
    return first_grad + inv_rms * scaled - first * (inv_rms * inv_rms * inv_rms) * inner


def local(acts, grads, in_proj, out_proj, gain):
    half = acts.shape[2] // 2
    dp_size = lax.axis_size("dp")
    tick_count = min(4, lax.axis_size("section") // 2)
    along_x, across_x = column_groups(dp_size)
    gain_row = gain[0]
    shard = jnp.concatenate([in_proj[0], out_proj[0]], axis=1)
    weights = copied_to_group(copied_to_group(shard, across_x), along_x)
    weight_in, weight_out = weights[:, :half], weights[:, half:]
    first, second = acts[0, :, :half], acts[0, :, half:]
    first_grad, second_grad = grads[0, :, :half], grads[0, :, half:]
    hiddens, cotangents = [], []
    for tick_index in range(tick_count):
        inv_rms, hidden, slopes, new_first = forward(first, second, gain_row, weight_in, weight_out)
        acts_pair = passed_back(
            jnp.concatenate([new_first, first], axis=1).astype(jnp.bfloat16)
        )
        cotangent = second_grad.astype(jnp.bfloat16)
        hiddens.append(hidden)
        cotangents.append(cotangent)
        new_second_grad = backward(
            first, inv_rms, slopes, cotangent, first_grad, gain_row, weight_in, weight_out
        )
        grads_pair = passed_back(
            jnp.concatenate([cotangent, new_second_grad.astype(jnp.bfloat16)], axis=1)
        )
        acts_pair = acts_pair.astype(jnp.float32)
        grads_pair = grads_pair.astype(jnp.float32)
        first, second = acts_pair[:, :half], acts_pair[:, half:]
        first_grad, second_grad = coupling_scale * grads_pair[:, :half], grads_pair[:, half:]
    outer = lax.dot_general(
        jnp.concatenate(hiddens, axis=0),
        jnp.concatenate(cotangents, axis=0),
        (((0,), (0,)), ((), ())),
        preferred_element_type=jnp.float32,
    ).astype(jnp.bfloat16)
    parts = exchanged(outer, along_x).reshape(x_size, -1, half)
    parts = jnp.sum(parts.astype(jnp.float32), axis=0).astype(jnp.bfloat16)
    parts = exchanged(parts, across_x).reshape(dp_size // x_size, -1, half)
    share = jnp.sum(parts.astype(jnp.float32), axis=0)
    grads_out = jnp.concatenate([first_grad, second_grad], axis=1)
    return (acts_pair[None], grads_out[None], share[None])


def solution(mesh):
    pair = P("section", "dp", None)
    return jax.shard_map(
        local,
        mesh=mesh,
        in_specs=(pair, pair, pair, pair, P("section", None)),
        out_specs=(pair, pair, pair),
        check_vma=False,
    )
```

```python
import functools

import jax
import jax.numpy as jnp
from jax import lax
from jax.experimental import pallas as pl
from jax.experimental.pallas import tpu as pltpu
from jax.sharding import PartitionSpec as P

coupling_scale = 32.0**0.25
rms_epsilon = 1e-06
root_half = 0.7071067811865476
inv_root_two_pi = 0.3989422804014327

x_size = 4
pair_size = 2


def dp_index(z, x, y):
    return (z * x_size + x) * pair_size + y


def z_size():
    return lax.axis_size("dp") // (x_size * pair_size)


def along_z():
    return [
        [dp_index(z, x, y) for z in range(z_size())]
        for x in range(x_size)
        for y in range(pair_size)
    ]


def across_x():
    return [
        [dp_index(z, x, y) for z in range(z_size()) for y in range(pair_size)]
        for x in range(x_size)
    ]


def shifted(block, x_step, y_step=0):
    route = [
        (dp_index(z, (x + x_step) % x_size, (y + y_step) % pair_size), dp_index(z, x, y))
        for z in range(z_size())
        for x in range(x_size)
        for y in range(pair_size)
    ]
    return lax.ppermute(block, "dp", route)


def exchanged(blocks, groups):
    return lax.all_to_all(blocks, "dp", 0, 0, axis_index_groups=groups, tiled=True)


def passed_back(block):
    devices = range(lax.axis_size("section"))
    return lax.ppermute(block, "section", [(i, i - 1) for i in devices if i])


def gathered_along_z(shard):
    return exchanged(jnp.tile(shard, (z_size(), 1)), along_z())


def gathered_along_x(block):
    rows = block.shape[0] // 2
    left, right = shifted(block, -1), shifted(block, 1)
    far_head = shifted(left[:rows], -1)
    far_tail = shifted(right[rows:], 1)
    return block, left, right, far_head, far_tail


def local_copies(weight_refs, weights, sems):
    copies, offset = [], 0
    for i, ref in enumerate(weight_refs):
        rows = ref.shape[0]
        copies.append(
            pltpu.make_async_copy(ref, weights.at[pl.ds(offset, rows)], sems.at[i])
        )
        offset += rows
    for copy in copies:
        copy.start()
    return copies


def forward_kernel(count, acts_ref, gain_ref, *refs):
    weight_refs, (hidden_ref, slopes_ref, acts_out_ref, weights, sems) = refs[:count], refs[count:]
    half = acts_ref.shape[1] // 2
    copies = local_copies(weight_refs, weights, sems)
    first = acts_ref[:, :half].astype(jnp.float32)
    inv_rms = lax.rsqrt(jnp.mean(first * first, axis=-1, keepdims=True) + rms_epsilon)
    normed = (first * inv_rms * gain_ref[...]).astype(jnp.bfloat16)
    offset = 0
    for copy, ref in zip(copies, weight_refs):
        rows = ref.shape[0]
        span = pl.ds(offset, rows)
        copy.wait()
        preact = lax.dot_general(
            normed,
            weights[span, :half],
            (((1,), (1,)), ((), ())),
            preferred_element_type=jnp.float32,
        )
        normal_cdf = 0.5 * (1.0 + lax.erf(preact * root_half))
        density = jnp.exp(-0.5 * preact * preact) * inv_root_two_pi
        hidden_ref[:, span] = (preact * normal_cdf).astype(jnp.bfloat16)
        slopes_ref[:, span] = (normal_cdf + preact * density).astype(slopes_ref.dtype)
        offset += rows
    branch = jnp.dot(hidden_ref[...], weights[:, half:], preferred_element_type=jnp.float32)
    second = acts_ref[:, half:].astype(jnp.float32)
    acts_out_ref[:, :half] = ((second - branch) / coupling_scale).astype(jnp.bfloat16)
    acts_out_ref[:, half:] = first.astype(jnp.bfloat16)


def backward_kernel(count, scale, acts_ref, grads_ref, gain_ref, slopes_ref, *refs):
    weight_refs, (grads_out_ref, pre_grad, weights, sems) = refs[:count], refs[count:]
    half = acts_ref.shape[1] // 2
    copies = local_copies(weight_refs, weights, sems)
    cotangent = grads_ref[:, half:].astype(jnp.bfloat16)
    offset = 0
    for copy, ref in zip(copies, weight_refs):
        rows = ref.shape[0]
        span = pl.ds(offset, rows)
        copy.wait()
        hidden_grad = lax.dot_general(
            cotangent,
            weights[span, half:],
            (((1,), (1,)), ((), ())),
            preferred_element_type=jnp.float32,
        )
        slopes = slopes_ref[:, span].astype(jnp.float32)
        pre_grad[:, span] = (hidden_grad * slopes).astype(jnp.bfloat16)
        offset += rows
    norm_grad = jnp.dot(pre_grad[...], weights[:, :half], preferred_element_type=jnp.float32)
    first = acts_ref[:, :half].astype(jnp.float32)
    inv_rms = lax.rsqrt(jnp.mean(first * first, axis=-1, keepdims=True) + rms_epsilon)
    scaled = norm_grad * gain_ref[...]
    inner = jnp.mean(first * scaled, axis=-1, keepdims=True)
    input_grad = inv_rms * scaled - first * (inv_rms * inv_rms * inv_rms) * inner
    first_grad = grads_ref[:, :half].astype(jnp.float32)
    if scale != 1.0:
        first_grad = first_grad * scale
    grads_out_ref[:, :half] = cotangent
    grads_out_ref[:, half:] = (first_grad + input_grad).astype(jnp.bfloat16)


def scratch(weights, *more):
    rows = sum(w.shape[0] for w in weights)
    return [
        *more,
        pltpu.VMEM((rows, weights[0].shape[1]), jnp.bfloat16),
        pltpu.SemaphoreType.DMA((len(weights),)),
    ]


def in_vmem(count):
    return [pl.BlockSpec(memory_space=pltpu.VMEM)] * count


def cost(tokens, units, half):
    return pl.CostEstimate(
        flops=4 * tokens * units * half,
        bytes_accessed=4 * units * half + 4 * tokens * units,
        transcendentals=2 * tokens * units,
    )


def forward(acts, gain, weights):
    tokens, width = acts.shape
    units = sum(w.shape[0] for w in weights)
    return pl.pallas_call(
        functools.partial(forward_kernel, len(weights)),
        out_shape=(
            jax.ShapeDtypeStruct((tokens, units), jnp.bfloat16),
            jax.ShapeDtypeStruct((tokens, units), jnp.bfloat16),
            jax.ShapeDtypeStruct((tokens, width), jnp.bfloat16),
        ),
        in_specs=in_vmem(2) + [pl.BlockSpec(memory_space=pl.ANY)] * len(weights),
        out_specs=tuple(in_vmem(3)),
        scratch_shapes=scratch(weights),
        cost_estimate=cost(tokens, units, width // 2),
        compiler_params=pltpu.CompilerParams(vmem_limit_bytes=24 * 2**20),
        name="forward_half",
    )(acts, gain, *weights)


def backward(scale, acts, grads, gain, slopes, weights):
    tokens, width = acts.shape
    units = slopes.shape[1]
    return pl.pallas_call(
        functools.partial(backward_kernel, len(weights), scale),
        out_shape=jax.ShapeDtypeStruct((tokens, width), jnp.bfloat16),
        in_specs=in_vmem(4) + [pl.BlockSpec(memory_space=pl.ANY)] * len(weights),
        out_specs=in_vmem(1)[0],
        scratch_shapes=scratch(weights, pltpu.VMEM((tokens, units), jnp.bfloat16)),
        cost_estimate=cost(tokens, units, width // 2),
        compiler_params=pltpu.CompilerParams(vmem_limit_bytes=24 * 2**20),
        name="backward_half",
    )(acts, grads, gain, slopes, *weights)


def outer_rows(hidden, cotangent, start, count):
    rows = lax.slice_in_dim(hidden, start, start + count, axis=1)
    return lax.dot_general(
        rows, cotangent, (((0,), (0,)), ((), ())), preferred_element_type=jnp.float32
    ).astype(jnp.bfloat16)


def local(acts, grads, in_proj, out_proj, gain):
    half = acts.shape[2] // 2
    tick_count = min(4, lax.axis_size("section") // 2)
    shard = jnp.concatenate([in_proj[0], out_proj[0]], axis=1)
    partner_shard = shifted(shard, 0, 1)
    near = gathered_along_x(gathered_along_z(shard))
    far = gathered_along_x(gathered_along_z(partner_shard))
    own_n, left_n, right_n, head_n, tail_n = near
    own_f, left_f, right_f, head_f, tail_f = far
    weights = (own_n, own_f, left_n, left_f, right_n, right_f, head_n, tail_n, head_f, tail_f)
    quarter = own_n.shape[0] * 2

    acts_pair, grads_pair, scale = acts[0], grads[0], 1.0
    hiddens, cotangents = [], []
    for tick_index in range(tick_count):
        hidden, slopes, new_acts = forward(acts_pair, gain, weights)
        next_acts = passed_back(new_acts)
        new_grads = backward(scale, acts_pair, grads_pair, gain, slopes, weights)
        hiddens.append(hidden)
        cotangents.append(new_grads[:, :half])
        acts_pair, grads_pair, scale = next_acts, passed_back(new_grads), coupling_scale

    hidden, cotangent = jnp.concatenate(hiddens, axis=0), jnp.concatenate(cotangents, axis=0)
    far_x = shifted(outer_rows(hidden, cotangent, 3 * quarter, quarter), 2)
    from_right = shifted(outer_rows(hidden, cotangent, quarter, quarter), 1)
    from_left = shifted(outer_rows(hidden, cotangent, 2 * quarter, quarter), -1)
    own = outer_rows(hidden, cotangent, 0, quarter)
    total = (
        own.astype(jnp.float32)
        + from_right.astype(jnp.float32)
        + from_left.astype(jnp.float32)
        + far_x.astype(jnp.float32)
    ).astype(jnp.bfloat16)
    y_hi = lax.axis_index("dp") % pair_size
    mine, other = total[: quarter // 2], total[quarter // 2 :]
    low, high = jnp.where(y_hi == 0, mine, other), jnp.where(y_hi == 0, other, mine)
    units = in_proj.shape[1]
    blocks = jnp.stack([low.reshape(-1, units, half), high.reshape(-1, units, half)], axis=1)
    parts = exchanged(blocks.reshape(-1, half), across_x()).reshape(-1, units, half)
    share = jnp.sum(parts.astype(jnp.float32), axis=0)

    grads_pair = grads_pair.astype(jnp.float32)
    grads_out = jnp.concatenate(
        [coupling_scale * grads_pair[:, :half], grads_pair[:, half:]], axis=1
    )
    return (acts_pair.astype(jnp.float32)[None], grads_out[None], share[None])


def solution(mesh):
    pair = P("section", "dp", None)
    return jax.shard_map(
        local,
        mesh=mesh,
        in_specs=(pair, pair, pair, pair, P("section", None)),
        out_specs=(pair, pair, pair),
        check_vma=False,
    )
```

```python
import functools

import jax
import jax.numpy as jnp
from jax import lax
from jax.experimental import pallas as pl
from jax.experimental.pallas import tpu as pltpu
from jax.sharding import PartitionSpec as P

coupling_scale = 32.0**0.25
rms_epsilon = 1e-06
root_half = 0.7071067811865476
inv_root_two_pi = 0.3989422804014327

x_size = 4
pair_size = 2


def dp_index(z, x, y):
    return (z * x_size + x) * pair_size + y


def z_size():
    return lax.axis_size("dp") // (x_size * pair_size)


def along_z():
    return [
        [dp_index(z, x, y) for z in range(z_size())]
        for x in range(x_size)
        for y in range(pair_size)
    ]


def across_x():
    return [
        [dp_index(z, x, y) for z in range(z_size()) for y in range(pair_size)]
        for x in range(x_size)
    ]


def shifted(block, x_step, y_step=0):
    route = [
        (dp_index(z, (x + x_step) % x_size, (y + y_step) % pair_size), dp_index(z, x, y))
        for z in range(z_size())
        for x in range(x_size)
        for y in range(pair_size)
    ]
    return lax.ppermute(block, "dp", route)


def exchanged(blocks, groups):
    return lax.all_to_all(blocks, "dp", 0, 0, axis_index_groups=groups, tiled=True)


def passed_back(block):
    devices = range(lax.axis_size("section"))
    return lax.ppermute(block, "section", [(i, i - 1) for i in devices if i])


def gathered_along_z(shard):
    return exchanged(jnp.tile(shard, (z_size(), 1)), along_z())


def gathered_along_x(block):
    rows = block.shape[0] // 2
    left, right = shifted(block, -1), shifted(block, 1)
    far_head = shifted(left[:rows], -1)
    far_tail = shifted(right[rows:], 1)
    return block, left, right, far_head, far_tail


def forward_kernel(acts_ref, gain_ref, *refs):
    weight_refs, (hidden_ref, slopes_ref, acts_out_ref) = refs[:-3], refs[-3:]
    half = acts_ref.shape[1] // 2
    first = acts_ref[:, :half].astype(jnp.float32)
    inv_rms = lax.rsqrt(jnp.mean(first * first, axis=-1, keepdims=True) + rms_epsilon)
    normed = (first * inv_rms * gain_ref[...]).astype(jnp.bfloat16)
    for span, weight_ref in spans(weight_refs):
        preact = lax.dot_general(
            normed,
            weight_ref[:, :half],
            (((1,), (1,)), ((), ())),
            preferred_element_type=jnp.float32,
        )
        normal_cdf = 0.5 * (1.0 + lax.erf(preact * root_half))
        density = jnp.exp(-0.5 * preact * preact) * inv_root_two_pi
        hidden_ref[:, span] = (preact * normal_cdf).astype(jnp.bfloat16)
        slopes_ref[:, span] = (normal_cdf + preact * density).astype(slopes_ref.dtype)
    branch = sum(
        jnp.dot(hidden_ref[:, span], weight_ref[:, half:], preferred_element_type=jnp.float32)
        for span, weight_ref in spans(weight_refs)
    )
    second = acts_ref[:, half:].astype(jnp.float32)
    acts_out_ref[:, :half] = ((second - branch) / coupling_scale).astype(jnp.bfloat16)
    acts_out_ref[:, half:] = first.astype(jnp.bfloat16)


def backward_kernel(scale, acts_ref, grads_ref, gain_ref, slopes_ref, *refs):
    weight_refs, (grads_out_ref, pre_grad) = refs[:-2], refs[-2:]
    half = acts_ref.shape[1] // 2
    cotangent = grads_ref[:, half:].astype(jnp.bfloat16)
    for span, weight_ref in spans(weight_refs):
        hidden_grad = lax.dot_general(
            cotangent,
            weight_ref[:, half:],
            (((1,), (1,)), ((), ())),
            preferred_element_type=jnp.float32,
        )
        slopes = slopes_ref[:, span].astype(jnp.float32)
        pre_grad[:, span] = (hidden_grad * slopes).astype(jnp.bfloat16)
    norm_grad = sum(
        jnp.dot(pre_grad[:, span], weight_ref[:, :half], preferred_element_type=jnp.float32)
        for span, weight_ref in spans(weight_refs)
    )
    first = acts_ref[:, :half].astype(jnp.float32)
    inv_rms = lax.rsqrt(jnp.mean(first * first, axis=-1, keepdims=True) + rms_epsilon)
    scaled = norm_grad * gain_ref[...]
    inner = jnp.mean(first * scaled, axis=-1, keepdims=True)
    input_grad = inv_rms * scaled - first * (inv_rms * inv_rms * inv_rms) * inner
    first_grad = grads_ref[:, :half].astype(jnp.float32)
    if scale != 1.0:
        first_grad = first_grad * scale
    grads_out_ref[:, :half] = cotangent
    grads_out_ref[:, half:] = (first_grad + input_grad).astype(jnp.bfloat16)


def outer_kernel(start, columns, *refs):
    ticks = len(columns)
    hidden_refs, cotangent_refs, out_ref = refs[:ticks], refs[ticks:-1], refs[-1]
    count, half = out_ref.shape
    rows = jnp.concatenate([ref[:, start : start + count] for ref in hidden_refs], axis=0)
    cotangents = jnp.concatenate(
        [ref[:, at : at + half] for ref, at in zip(cotangent_refs, columns)], axis=0
    )
    total = lax.dot_general(
        rows, cotangents, (((0,), (0,)), ((), ())), preferred_element_type=jnp.float32
    )
    out_ref[...] = total.astype(out_ref.dtype)


def spans(weight_refs):
    offset = 0
    for ref in weight_refs:
        yield pl.ds(offset, ref.shape[0]), ref
        offset += ref.shape[0]


def in_vmem(count):
    return [pl.BlockSpec(memory_space=pltpu.VMEM)] * count


def cost(tokens, units, half):
    return pl.CostEstimate(
        flops=4 * tokens * units * half,
        bytes_accessed=4 * units * half + 4 * tokens * units,
        transcendentals=2 * tokens * units,
    )


def kernel_params():
    return pltpu.CompilerParams(vmem_limit_bytes=16 * 2**20)


def forward(acts, gain, weights):
    tokens, width = acts.shape
    units = sum(w.shape[0] for w in weights)
    return pl.pallas_call(
        forward_kernel,
        out_shape=(
            jax.ShapeDtypeStruct((tokens, units), jnp.bfloat16),
            jax.ShapeDtypeStruct((tokens, units), jnp.bfloat16),
            jax.ShapeDtypeStruct((tokens, width), jnp.bfloat16),
        ),
        in_specs=in_vmem(2 + len(weights)),
        out_specs=tuple(in_vmem(3)),
        cost_estimate=cost(tokens, units, width // 2),
        compiler_params=kernel_params(),
        name="forward_half",
    )(acts, gain, *weights)


def backward(scale, acts, grads, gain, slopes, weights):
    tokens, width = acts.shape
    units = slopes.shape[1]
    return pl.pallas_call(
        functools.partial(backward_kernel, scale),
        out_shape=jax.ShapeDtypeStruct((tokens, width), jnp.bfloat16),
        in_specs=in_vmem(4 + len(weights)),
        out_specs=in_vmem(1)[0],
        scratch_shapes=[pltpu.VMEM((tokens, units), jnp.bfloat16)],
        cost_estimate=cost(tokens, units, width // 2),
        compiler_params=kernel_params(),
        name="backward_half",
    )(acts, grads, gain, slopes, *weights)


def outer_rows(hiddens, cotangents, columns, start, count):
    half = cotangents[0].shape[1] // 2
    tokens = hiddens[0].shape[0] * len(hiddens)
    return pl.pallas_call(
        functools.partial(outer_kernel, start, columns),
        out_shape=jax.ShapeDtypeStruct((count, half), jnp.bfloat16),
        in_specs=in_vmem(2 * len(hiddens)),
        out_specs=in_vmem(1)[0],
        cost_estimate=pl.CostEstimate(
            flops=2 * tokens * count * half,
            bytes_accessed=2 * (tokens * count + tokens * half + count * half),
            transcendentals=0,
        ),
        compiler_params=kernel_params(),
        name="outer_rows",
    )(*hiddens, *cotangents)


def local(acts, grads, in_proj, out_proj, gain):
    half = acts.shape[2] // 2
    tick_count = min(4, lax.axis_size("section") // 2)
    is_low = (lax.axis_index("dp") & (pair_size - 1)) == 0
    shard = jnp.concatenate([in_proj[0], out_proj[0]], axis=1)
    shard, is_low = lax.optimization_barrier((shard, is_low))
    partner_shard = shifted(shard, 0, 1)
    near = gathered_along_x(gathered_along_z(shard))
    far = gathered_along_x(gathered_along_z(partner_shard))
    own_n, left_n, right_n, head_n, tail_n = near
    own_f, left_f, right_f, head_f, tail_f = far
    weights = (own_n, own_f, left_n, left_f, right_n, right_f, head_n, tail_n, head_f, tail_f)
    quarter = own_n.shape[0] * 2

    acts_pair, grads_pair, scale = acts[0], grads[0], 1.0
    hiddens, cotangents, columns = [], [], []
    for tick_index in range(tick_count):
        hidden, slopes, new_acts = forward(acts_pair, gain, weights)
        next_acts = passed_back(new_acts)
        hiddens.append(hidden)
        if tick_index == tick_count - 1:
            cotangents.append(grads_pair)
            columns.append(half)
            parts = [
                outer_rows(hiddens, cotangents, columns, i * quarter, quarter) for i in (3, 1, 2)
            ]
            far_x = shifted(parts[0], 2)
            from_right = shifted(parts[1], 1)
            from_left = shifted(parts[2], -1)
            acts_pair, grads_pair, _ = lax.optimization_barrier(
                (acts_pair, grads_pair, parts)
            )
        new_grads = backward(scale, acts_pair, grads_pair, gain, slopes, weights)
        if tick_index < tick_count - 1:
            cotangents.append(new_grads)
            columns.append(0)
        acts_pair, grads_pair, scale = next_acts, passed_back(new_grads), coupling_scale

    own = outer_rows(hiddens, cotangents, columns, 0, quarter)
    total = (
        own.astype(jnp.float32)
        + from_right.astype(jnp.float32)
        + from_left.astype(jnp.float32)
        + far_x.astype(jnp.float32)
    ).astype(jnp.bfloat16)
    mine, other = total[: quarter // 2], total[quarter // 2 :]
    low, high = jnp.where(is_low, mine, other), jnp.where(is_low, other, mine)
    units = in_proj.shape[1]
    blocks = jnp.stack([low.reshape(-1, units, half), high.reshape(-1, units, half)], axis=1)
    blocks, acts_pair, grads_pair = lax.optimization_barrier(
        (blocks.reshape(-1, half), acts_pair, grads_pair)
    )
    parts = exchanged(blocks, across_x()).reshape(-1, units, half)
    share = jnp.sum(parts.astype(jnp.float32), axis=0)

    grads_pair = grads_pair.astype(jnp.float32)
    grads_out = jnp.concatenate(
        [coupling_scale * grads_pair[:, :half], grads_pair[:, half:]], axis=1
    )
    return (acts_pair.astype(jnp.float32)[None], grads_out[None], share[None])


def solution(mesh):
    pair = P("section", "dp", None)
    return jax.shard_map(
        local,
        mesh=mesh,
        in_specs=(pair, pair, pair, pair, P("section", None)),
        out_specs=(pair, pair, pair),
        check_vma=False,
    )
```

```python
import functools

import jax
import jax.numpy as jnp
from jax import lax
from jax.experimental import pallas as pl
from jax.experimental.pallas import tpu as pltpu
from jax.sharding import PartitionSpec as P

coupling_scale = 32.0**0.25
rms_epsilon = 1e-06
root_half = 0.7071067811865476
inv_root_two_pi = 0.3989422804014327

x_size = 4
pair_size = 2


def dp_index(z, x, y):
    return (z * x_size + x) * pair_size + y


def z_size():
    return lax.axis_size("dp") // (x_size * pair_size)


def along_z():
    return [
        [dp_index(z, x, y) for z in range(z_size())]
        for x in range(x_size)
        for y in range(pair_size)
    ]


def across_x():
    return [
        [dp_index(z, x, y) for z in range(z_size()) for y in range(pair_size)]
        for x in range(x_size)
    ]


def swapped(block, peer_x=lambda x: x, peer_y=lambda y: y):
    route = [
        (dp_index(z, peer_x(x), peer_y(y)), dp_index(z, x, y))
        for z in range(z_size())
        for x in range(x_size)
        for y in range(pair_size)
    ]
    return lax.ppermute(block, "dp", route)


def near_x(x):
    return x ^ 1


def next_x(x):
    return (x + 1 if x % 2 else x - 1) % x_size


def far_x(x):
    return (x + 2) % x_size


def other_y(y):
    return 1 - y


def exchanged(blocks, groups):
    return lax.all_to_all(blocks, "dp", 0, 0, axis_index_groups=groups, tiled=True)


def passed_back(block):
    devices = range(lax.axis_size("section"))
    return lax.ppermute(block, "section", [(i, i - 1) for i in devices if i])


def gathered_along_z(shard):
    return exchanged(jnp.tile(shard, (z_size(), 1)), along_z())


def gathered_along_x(block):
    rows = block.shape[0] // 2
    near, following = swapped(block, near_x), swapped(block, next_x)
    far_head = swapped(following[:rows], near_x)
    far_tail = swapped(near[rows:], next_x)
    return block, near, following, far_head, far_tail


def forward_kernel(acts_ref, gain_ref, *refs):
    weight_refs, (hidden_ref, slopes_ref, acts_out_ref) = refs[:-3], refs[-3:]
    half = acts_ref.shape[1] // 2
    first = acts_ref[:, :half].astype(jnp.float32)
    inv_rms = lax.rsqrt(jnp.mean(first * first, axis=-1, keepdims=True) + rms_epsilon)
    normed = (first * inv_rms * gain_ref[...]).astype(jnp.bfloat16)
    for span, weight_ref in spans(weight_refs):
        preact = lax.dot_general(
            normed,
            weight_ref[:, :half],
            (((1,), (1,)), ((), ())),
            preferred_element_type=jnp.float32,
        )
        normal_cdf = 0.5 * (1.0 + lax.erf(preact * root_half))
        density = jnp.exp(-0.5 * preact * preact) * inv_root_two_pi
        hidden_ref[:, span] = (preact * normal_cdf).astype(jnp.bfloat16)
        slopes_ref[:, span] = (normal_cdf + preact * density).astype(slopes_ref.dtype)
    branch = sum(
        jnp.dot(hidden_ref[:, span], weight_ref[:, half:], preferred_element_type=jnp.float32)
        for span, weight_ref in spans(weight_refs)
    )
    second = acts_ref[:, half:].astype(jnp.float32)
    acts_out_ref[:, :half] = ((second - branch) / coupling_scale).astype(jnp.bfloat16)
    acts_out_ref[:, half:] = first.astype(jnp.bfloat16)


def backward_kernel(scale, acts_ref, grads_ref, gain_ref, slopes_ref, *refs):
    weight_refs, (grads_out_ref, pre_grad) = refs[:-2], refs[-2:]
    half = acts_ref.shape[1] // 2
    cotangent = grads_ref[:, half:].astype(jnp.bfloat16)
    for span, weight_ref in spans(weight_refs):
        hidden_grad = lax.dot_general(
            cotangent,
            weight_ref[:, half:],
            (((1,), (1,)), ((), ())),
            preferred_element_type=jnp.float32,
        )
        slopes = slopes_ref[:, span].astype(jnp.float32)
        pre_grad[:, span] = (hidden_grad * slopes).astype(jnp.bfloat16)
    norm_grad = sum(
        jnp.dot(pre_grad[:, span], weight_ref[:, :half], preferred_element_type=jnp.float32)
        for span, weight_ref in spans(weight_refs)
    )
    first = acts_ref[:, :half].astype(jnp.float32)
    inv_rms = lax.rsqrt(jnp.mean(first * first, axis=-1, keepdims=True) + rms_epsilon)
    scaled = norm_grad * gain_ref[...]
    inner = jnp.mean(first * scaled, axis=-1, keepdims=True)
    input_grad = inv_rms * scaled - first * (inv_rms * inv_rms * inv_rms) * inner
    first_grad = grads_ref[:, :half].astype(jnp.float32)
    if scale != 1.0:
        first_grad = first_grad * scale
    grads_out_ref[:, :half] = cotangent
    grads_out_ref[:, half:] = (first_grad + input_grad).astype(jnp.bfloat16)


def outer_kernel(start, columns, *refs):
    ticks = len(columns)
    hidden_refs, cotangent_refs, out_ref = refs[:ticks], refs[ticks:-1], refs[-1]
    count, half = out_ref.shape
    rows = jnp.concatenate([ref[:, start : start + count] for ref in hidden_refs], axis=0)
    cotangents = jnp.concatenate(
        [ref[:, at : at + half] for ref, at in zip(cotangent_refs, columns)], axis=0
    )
    total = lax.dot_general(
        rows, cotangents, (((0,), (0,)), ((), ())), preferred_element_type=jnp.float32
    )
    out_ref[...] = total.astype(out_ref.dtype)


def combine_kernel(y_ref, own_ref, near_ref, next_ref, far_ref, out_ref):
    units = out_ref.shape[2]
    half_rows = own_ref.shape[0] // 2
    for part in range(pair_size):
        rows = pl.ds(part * half_rows, half_rows)
        total = (
            own_ref[rows, :].astype(jnp.float32)
            + near_ref[rows, :].astype(jnp.float32)
            + next_ref[rows, :].astype(jnp.float32)
            + far_ref[rows, :].astype(jnp.float32)
        ).astype(out_ref.dtype)
        blocks = total.reshape(-1, units, total.shape[1])
        for y in range(pair_size):

            @pl.when(y_ref[0] == y)
            def _():
                out_ref[:, y if part == 0 else 1 - y] = blocks


def spans(weight_refs):
    offset = 0
    for ref in weight_refs:
        yield pl.ds(offset, ref.shape[0]), ref
        offset += ref.shape[0]


def in_vmem(count):
    return [pl.BlockSpec(memory_space=pltpu.VMEM)] * count


def cost(tokens, units, half):
    return pl.CostEstimate(
        flops=4 * tokens * units * half,
        bytes_accessed=4 * units * half + 4 * tokens * units,
        transcendentals=2 * tokens * units,
    )


def kernel_params():
    return pltpu.CompilerParams(vmem_limit_bytes=16 * 2**20)


def forward(acts, gain, weights):
    tokens, width = acts.shape
    units = sum(w.shape[0] for w in weights)
    return pl.pallas_call(
        forward_kernel,
        out_shape=(
            jax.ShapeDtypeStruct((tokens, units), jnp.bfloat16),
            jax.ShapeDtypeStruct((tokens, units), jnp.bfloat16),
            jax.ShapeDtypeStruct((tokens, width), jnp.bfloat16),
        ),
        in_specs=in_vmem(2 + len(weights)),
        out_specs=tuple(in_vmem(3)),
        cost_estimate=cost(tokens, units, width // 2),
        compiler_params=kernel_params(),
        name="forward_half",
    )(acts, gain, *weights)


def backward(scale, acts, grads, gain, slopes, weights):
    tokens, width = acts.shape
    units = slopes.shape[1]
    return pl.pallas_call(
        functools.partial(backward_kernel, scale),
        out_shape=jax.ShapeDtypeStruct((tokens, width), jnp.bfloat16),
        in_specs=in_vmem(4 + len(weights)),
        out_specs=in_vmem(1)[0],
        scratch_shapes=[pltpu.VMEM((tokens, units), jnp.bfloat16)],
        cost_estimate=cost(tokens, units, width // 2),
        compiler_params=kernel_params(),
        name="backward_half",
    )(acts, grads, gain, slopes, *weights)


def outer_rows(hiddens, cotangents, columns, start, count):
    half = cotangents[0].shape[1] // 2
    tokens = hiddens[0].shape[0] * len(hiddens)
    return pl.pallas_call(
        functools.partial(outer_kernel, start, columns),
        out_shape=jax.ShapeDtypeStruct((count, half), jnp.bfloat16),
        in_specs=in_vmem(2 * len(hiddens)),
        out_specs=in_vmem(1)[0],
        cost_estimate=pl.CostEstimate(
            flops=2 * tokens * count * half,
            bytes_accessed=2 * (tokens * count + tokens * half + count * half),
            transcendentals=0,
        ),
        compiler_params=kernel_params(),
        name="outer_rows",
    )(*hiddens, *cotangents)


def combined(y_hi, units, parts):
    rows, half = parts[0].shape
    return pl.pallas_call(
        combine_kernel,
        out_shape=jax.ShapeDtypeStruct(
            (rows // (pair_size * units), pair_size, units, half), jnp.bfloat16
        ),
        in_specs=[pl.BlockSpec(memory_space=pltpu.SMEM)] + in_vmem(len(parts)),
        out_specs=in_vmem(1)[0],
        cost_estimate=pl.CostEstimate(
            flops=4 * rows * half, bytes_accessed=10 * rows * half, transcendentals=0
        ),
        compiler_params=kernel_params(),
        name="combine_parts",
    )(y_hi, *parts)


def local(acts, grads, in_proj, out_proj, gain):
    half = acts.shape[2] // 2
    tick_count = min(4, lax.axis_size("section") // 2)
    y_hi = (lax.axis_index("dp") & (pair_size - 1)).reshape(1)
    shard = jnp.concatenate([in_proj[0], out_proj[0]], axis=1)
    shard, y_hi = lax.optimization_barrier((shard, y_hi))
    partner_shard = swapped(shard, peer_y=other_y)
    near = gathered_along_x(gathered_along_z(shard))
    far = gathered_along_x(gathered_along_z(partner_shard))
    own_n, near_n, next_n, head_n, tail_n = near
    own_f, near_f, next_f, head_f, tail_f = far
    weights = (own_n, own_f, near_n, near_f, next_n, next_f, head_n, tail_n, head_f, tail_f)
    quarter = own_n.shape[0] * 2

    acts_pair, grads_pair, scale = acts[0], grads[0], 1.0
    hiddens, cotangents, columns = [], [], []
    for tick_index in range(tick_count):
        hidden, slopes, new_acts = forward(acts_pair, gain, weights)
        next_acts = passed_back(new_acts)
        hiddens.append(hidden)
        if tick_index == tick_count - 1:
            cotangents.append(grads_pair)
            columns.append(half)
            parts = [
                outer_rows(hiddens, cotangents, columns, i * quarter, quarter) for i in (3, 1, 2)
            ]
            from_far = swapped(parts[0], far_x)
            from_near = swapped(parts[1], near_x)
            from_next = swapped(parts[2], next_x)
            acts_pair, grads_pair, _ = lax.optimization_barrier(
                (acts_pair, grads_pair, parts)
            )
        new_grads = backward(scale, acts_pair, grads_pair, gain, slopes, weights)
        if tick_index < tick_count - 1:
            cotangents.append(new_grads)
            columns.append(0)
        acts_pair, grads_pair, scale = next_acts, passed_back(new_grads), coupling_scale

    own = outer_rows(hiddens, cotangents, columns, 0, quarter)
    units = in_proj.shape[1]
    blocks = combined(y_hi, units, (own, from_near, from_next, from_far))
    blocks, acts_pair, grads_pair = lax.optimization_barrier(
        (blocks.reshape(-1, half), acts_pair, grads_pair)
    )
    parts = exchanged(blocks, across_x()).reshape(-1, units, half)
    share = jnp.sum(parts.astype(jnp.float32), axis=0)

    grads_pair = grads_pair.astype(jnp.float32)
    grads_out = jnp.concatenate(
        [coupling_scale * grads_pair[:, :half], grads_pair[:, half:]], axis=1
    )
    return (acts_pair.astype(jnp.float32)[None], grads_out[None], share[None])


def solution(mesh):
    pair = P("section", "dp", None)
    return jax.shard_map(
        local,
        mesh=mesh,
        in_specs=(pair, pair, pair, pair, P("section", None)),
        out_specs=(pair, pair, pair),
        check_vma=False,
    )
```

```python
import functools

import jax
import jax.numpy as jnp
from jax import lax
from jax.experimental import pallas as pl
from jax.experimental.pallas import tpu as pltpu
from jax.sharding import PartitionSpec as P

coupling_scale = 32.0**0.25
rms_epsilon = 1e-06
root_half = 0.7071067811865476
inv_root_two_pi = 0.3989422804014327

x_size = 4
pair_size = 2


def dp_index(z, x, y):
    return (z * x_size + x) * pair_size + y


def z_size():
    return lax.axis_size("dp") // (x_size * pair_size)


def alike_groups():
    return [
        [
            dp_index(z, x, y)
            for z in range(parity, z_size(), 2)
            for y in range(pair_size)
        ]
        for parity in range(2)
        for x in range(x_size)
    ]


def swapped_along_x(block, peer):
    route = [
        (dp_index(z, peer(x), y), dp_index(z, x, y))
        for z in range(z_size())
        for x in range(x_size)
        for y in range(pair_size)
    ]
    return lax.ppermute(block, "dp", route)


def partner(index):
    return index ^ (x_size * pair_size)


def swapped_with_partner(block):
    return lax.ppermute(block, "dp", [(partner(i), i) for i in range(lax.axis_size("dp"))])


def near_x(x):
    return x ^ 1


def next_x(x):
    return (x + 1 if x % 2 else x - 1) % x_size


def far_x(x):
    return (x + 2) % x_size


def exchanged(blocks):
    return lax.all_to_all(
        blocks, "dp", 0, 0, axis_index_groups=alike_groups(), tiled=True
    )


def passed_back(block):
    devices = range(lax.axis_size("section"))
    return lax.ppermute(block, "section", [(i, i - 1) for i in devices if i])


def passed_back_to_partner(block):
    size = lax.axis_size("dp")
    route = [
        (section * size + i, (section - 1) * size + partner(i))
        for section in range(1, lax.axis_size("section"))
        for i in range(size)
    ]
    return lax.ppermute(block, ("section", "dp"), route)


def gathered_along_x(block):
    rows = block.shape[0] // 2
    near, following = swapped_along_x(block, near_x), swapped_along_x(block, next_x)
    far_head = swapped_along_x(following[:rows], near_x)
    far_tail = swapped_along_x(near[rows:], next_x)
    return block, near, following, far_head, far_tail


def inverse_rms(first):
    return lax.rsqrt(jnp.mean(first * first, axis=-1, keepdims=True) + rms_epsilon)


def forward_kernel(acts_ref, partner_ref, gain_ref, *refs):
    weight_refs, (hidden_ref, slopes_ref, kept_ref, sent_ref) = refs[:-4], refs[-4:]
    tokens, half = partner_ref.shape
    first = jnp.concatenate(
        [acts_ref[:, :half].astype(jnp.float32), partner_ref[...].astype(jnp.float32)], axis=0
    )
    normed = (first * inverse_rms(first) * gain_ref[...]).astype(jnp.bfloat16)
    for span, weight_ref in spans(weight_refs):
        preact = lax.dot_general(
            normed,
            weight_ref[:, :half],
            (((1,), (1,)), ((), ())),
            preferred_element_type=jnp.float32,
        )
        normal_cdf = 0.5 * (1.0 + lax.erf(preact * root_half))
        density = jnp.exp(-0.5 * preact * preact) * inv_root_two_pi
        hidden_ref[:, span] = (preact * normal_cdf).astype(jnp.bfloat16)
        slopes_ref[:, span] = (normal_cdf + preact * density).astype(slopes_ref.dtype)
    branch = sum(
        jnp.dot(hidden_ref[:, span], weight_ref[:, half:], preferred_element_type=jnp.float32)
        for span, weight_ref in spans(weight_refs)
    )
    kept_ref[...] = branch[:tokens]
    sent_ref[...] = branch[tokens:].astype(sent_ref.dtype)


def acts_kernel(acts_ref, kept_ref, received_ref, acts_out_ref, first_out_ref):
    half = kept_ref.shape[1]
    branch = kept_ref[...] + received_ref[...].astype(jnp.float32)
    second = acts_ref[:, half:].astype(jnp.float32)
    new_first = ((second - branch) / coupling_scale).astype(jnp.bfloat16)
    acts_out_ref[:, :half] = new_first
    acts_out_ref[:, half:] = acts_ref[:, :half].astype(jnp.bfloat16)
    first_out_ref[...] = new_first


def backward_kernel(grads_ref, partner_ref, slopes_ref, *refs):
    weight_refs, (kept_ref, sent_ref, pre_grad) = refs[:-3], refs[-3:]
    tokens, half = partner_ref.shape
    cotangent = jnp.concatenate(
        [grads_ref[:, half:].astype(jnp.bfloat16), partner_ref[...].astype(jnp.bfloat16)], axis=0
    )
    for span, weight_ref in spans(weight_refs):
        hidden_grad = lax.dot_general(
            cotangent,
            weight_ref[:, half:],
            (((1,), (1,)), ((), ())),
            preferred_element_type=jnp.float32,
        )
        slopes = slopes_ref[:, span].astype(jnp.float32)
        pre_grad[:, span] = (hidden_grad * slopes).astype(jnp.bfloat16)
    norm_grad = sum(
        jnp.dot(pre_grad[:, span], weight_ref[:, :half], preferred_element_type=jnp.float32)
        for span, weight_ref in spans(weight_refs)
    )
    kept_ref[...] = norm_grad[:tokens]
    sent_ref[...] = norm_grad[tokens:].astype(sent_ref.dtype)


def grads_kernel(
    scale, acts_ref, grads_ref, gain_ref, kept_ref, received_ref, grads_out_ref, second_out_ref
):
    half = kept_ref.shape[1]
    first = acts_ref[:, :half].astype(jnp.float32)
    inv_rms = inverse_rms(first)
    scaled = (kept_ref[...] + received_ref[...].astype(jnp.float32)) * gain_ref[...]
    inner = jnp.mean(first * scaled, axis=-1, keepdims=True)
    input_grad = inv_rms * scaled - first * (inv_rms * inv_rms * inv_rms) * inner
    first_grad = grads_ref[:, :half].astype(jnp.float32)
    if scale != 1.0:
        first_grad = first_grad * scale
    new_second = (first_grad + input_grad).astype(jnp.bfloat16)
    grads_out_ref[:, :half] = grads_ref[:, half:].astype(jnp.bfloat16)
    grads_out_ref[:, half:] = new_second
    second_out_ref[...] = new_second


def outer_kernel(start, columns, *refs):
    ticks = len(refs) // 3
    hidden_refs, cotangent_refs, out_ref = refs[:ticks], refs[ticks:-1], refs[-1]
    count, half = out_ref.shape
    rows = jnp.concatenate([ref[:, start : start + count] for ref in hidden_refs], axis=0)
    cotangents = jnp.concatenate(
        [ref[:, at : at + half] for ref, at in zip(cotangent_refs, columns)], axis=0
    )
    total = lax.dot_general(
        rows, cotangents, (((0,), (0,)), ((), ())), preferred_element_type=jnp.float32
    )
    out_ref[...] = total.astype(out_ref.dtype)


def spans(weight_refs):
    offset = 0
    for ref in weight_refs:
        yield pl.ds(offset, ref.shape[0]), ref
        offset += ref.shape[0]


def in_vmem(count):
    return [pl.BlockSpec(memory_space=pltpu.VMEM)] * count


def cost(tokens, units, half):
    return pl.CostEstimate(
        flops=4 * tokens * units * half,
        bytes_accessed=4 * units * half + 4 * tokens * units,
        transcendentals=2 * tokens * units,
    )


def kernel_params():
    return pltpu.CompilerParams(vmem_limit_bytes=16 * 2**20)


def call(kernel, name, cost_estimate, outs, operands, scratch=()):
    return pl.pallas_call(
        kernel,
        out_shape=tuple(jax.ShapeDtypeStruct(shape, dtype) for shape, dtype in outs),
        in_specs=in_vmem(len(operands)),
        out_specs=tuple(in_vmem(len(outs))),
        scratch_shapes=list(scratch),
        cost_estimate=cost_estimate,
        compiler_params=kernel_params(),
        name=name,
    )(*operands)


def forward(acts, partner_first, gain, weights):
    tokens, half = partner_first.shape
    units = sum(w.shape[0] for w in weights)
    return call(
        forward_kernel,
        "forward_half",
        cost(2 * tokens, units, half),
        (
            ((2 * tokens, units), jnp.bfloat16),
            ((2 * tokens, units), jnp.bfloat16),
            ((tokens, half), jnp.float32),
            ((tokens, half), jnp.bfloat16),
        ),
        (acts, partner_first, gain, *weights),
    )


def backward(grads, partner_cotangent, slopes, weights):
    tokens, half = partner_cotangent.shape
    units = slopes.shape[1]
    return call(
        backward_kernel,
        "backward_half",
        cost(2 * tokens, units, half),
        (((tokens, half), jnp.float32), ((tokens, half), jnp.bfloat16)),
        (grads, partner_cotangent, slopes, *weights),
        (pltpu.VMEM((2 * tokens, units), jnp.bfloat16),),
    )


def small_cost(tokens, half):
    return pl.CostEstimate(
        flops=16 * tokens * half, bytes_accessed=16 * tokens * half, transcendentals=0
    )


def new_acts_of(acts, kept, received):
    tokens, half = kept.shape
    return call(
        acts_kernel,
        "new_acts",
        small_cost(tokens, half),
        (((tokens, 2 * half), jnp.bfloat16), ((tokens, half), jnp.bfloat16)),
        (acts, kept, received),
    )


def new_grads_of(scale, acts, grads, gain, kept, received):
    tokens, half = kept.shape
    return call(
        functools.partial(grads_kernel, scale),
        "new_grads",
        small_cost(tokens, half),
        (((tokens, 2 * half), jnp.bfloat16), ((tokens, half), jnp.bfloat16)),
        (acts, grads, gain, kept, received),
    )


def outer_rows(hiddens, cotangents, columns, start, count, half):
    tokens = hiddens[0].shape[0] * len(hiddens)
    return call(
        functools.partial(outer_kernel, start, columns),
        "outer_rows",
        pl.CostEstimate(
            flops=2 * tokens * count * half,
            bytes_accessed=2 * (tokens * count + tokens * half + count * half),
            transcendentals=0,
        ),
        (((count, half), jnp.bfloat16),),
        (*hiddens, *cotangents),
    )[0]


def local(acts, grads, in_proj, out_proj, gain):
    half = acts.shape[2] // 2
    units = in_proj.shape[1]
    tick_count = min(4, lax.axis_size("section") // 2)
    shard = jnp.concatenate([in_proj[0], out_proj[0]], axis=1)
    group_size = len(alike_groups()[0])
    weights = gathered_along_x(exchanged(jnp.tile(shard, (group_size, 1))))
    quarter = group_size * units

    acts_pair, grads_pair, scale = acts[0], grads[0], 1.0
    partner_first = swapped_with_partner(acts_pair[:, :half])
    partner_cotangent = swapped_with_partner(grads_pair[:, half:].astype(jnp.bfloat16))
    hiddens, cotangents, columns = [], [], []
    for tick_index in range(tick_count):
        last = tick_index == tick_count - 1
        hidden, slopes, kept, sent = forward(acts_pair, partner_first, gain, weights)
        received = swapped_with_partner(sent)
        hiddens.append(hidden)
        if last:
            cotangents += [grads_pair, partner_cotangent]
            columns += [half, 0]
            parts = [
                outer_rows(hiddens, cotangents, columns, i * quarter, quarter, half)
                for i in (3, 1, 2)
            ]
            from_far = swapped_along_x(parts[0], far_x)
            from_near = swapped_along_x(parts[1], near_x)
            from_next = swapped_along_x(parts[2], next_x)
            acts_pair, grads_pair, _ = lax.optimization_barrier((acts_pair, grads_pair, parts))
        kept_grad, sent_grad = backward(grads_pair, partner_cotangent, slopes, weights)
        received_grad = swapped_with_partner(sent_grad)
        new_acts, new_first = new_acts_of(acts_pair, kept, received)
        next_acts = passed_back(new_acts)
        new_grads, new_second = new_grads_of(
            scale, acts_pair, grads_pair, gain, kept_grad, received_grad
        )
        next_grads = passed_back(new_grads)
        if not last:
            cotangents += [new_grads, partner_cotangent]
            columns += [0, 0]
            partner_first = passed_back_to_partner(new_first)
            partner_cotangent = passed_back_to_partner(new_second)
        acts_pair, grads_pair, scale = next_acts, next_grads, coupling_scale

    own = outer_rows(hiddens, cotangents, columns, 0, quarter, half)
    blocks = sum(x.astype(jnp.float32) for x in (own, from_near, from_next, from_far))
    blocks, acts_pair, grads_pair = lax.optimization_barrier(
        (blocks.astype(jnp.bfloat16), acts_pair, grads_pair)
    )
    parts = exchanged(blocks).reshape(-1, units, half)
    share = jnp.sum(parts.astype(jnp.float32), axis=0)

    grads_pair = grads_pair.astype(jnp.float32)
    grads_out = jnp.concatenate(
        [coupling_scale * grads_pair[:, :half], grads_pair[:, half:]], axis=1
    )
    return (acts_pair.astype(jnp.float32)[None], grads_out[None], share[None])


def solution(mesh):
    pair = P("section", "dp", None)
    return jax.shard_map(
        local,
        mesh=mesh,
        in_specs=(pair, pair, pair, pair, P("section", None)),
        out_specs=(pair, pair, pair),
        check_vma=False,
    )
```

```python
import functools

import jax
import jax.numpy as jnp
from jax import lax
from jax.experimental import pallas as pl
from jax.experimental.pallas import tpu as pltpu
from jax.sharding import PartitionSpec as P


coupling_scale = 32.0**0.25
rms_epsilon = 1e-06
root_half = 0.7071067811865476
inv_root_two_pi = 0.3989422804014327

x_size = 4
pair_size = 2


def dp_index(z, x, y):
    return (z * x_size + x) * pair_size + y


def z_size():
    return lax.axis_size("dp") // (x_size * pair_size)


def alike_groups():
    return [
        [
            dp_index(z, x, y)
            for z in range(parity, z_size(), 2)
            for y in range(pair_size)
        ]
        for parity in range(2)
        for x in range(x_size)
    ]


def swapped_along_x(block, peer):
    route = [
        (dp_index(z, peer(x), y), dp_index(z, x, y))
        for z in range(z_size())
        for x in range(x_size)
        for y in range(pair_size)
    ]
    return lax.ppermute(block, "dp", route)


def partner(index):
    return index ^ (x_size * pair_size)


def swapped_with_partner(block):
    return lax.ppermute(block, "dp", [(partner(i), i) for i in range(lax.axis_size("dp"))])


def near_x(x):
    return x ^ 1


def next_x(x):
    return (x + 1 if x % 2 else x - 1) % x_size


def far_x(x):
    return (x + 2) % x_size


def exchanged(blocks):
    return lax.all_to_all(
        blocks, "dp", 0, 0, axis_index_groups=alike_groups(), tiled=True
    )


def passed_back(block):
    devices = range(lax.axis_size("section"))
    return lax.ppermute(block, "section", [(i, i - 1) for i in devices if i])


def passed_back_to_partner(block):
    size = lax.axis_size("dp")
    route = [
        (section * size + i, (section - 1) * size + partner(i))
        for section in range(1, lax.axis_size("section"))
        for i in range(size)
    ]
    return lax.ppermute(block, ("section", "dp"), route)


def gathered_along_x(block):
    rows = block.shape[0] // 2
    near, following = swapped_along_x(block, near_x), swapped_along_x(block, next_x)
    far_head = swapped_along_x(following[:rows], near_x)
    far_tail = swapped_along_x(near[rows:], next_x)
    return block, near, following, far_head, far_tail


def inverse_rms(first):
    return lax.rsqrt(jnp.mean(first * first, axis=-1, keepdims=True) + rms_epsilon)


def forward_kernel(acts_ref, partner_ref, gain_ref, *refs):
    weight_refs, (hidden_ref, slopes_ref, kept_ref, sent_ref) = refs[:-4], refs[-4:]
    tokens, half = partner_ref.shape
    first = jnp.concatenate(
        [acts_ref[:, :half].astype(jnp.float32), partner_ref[...].astype(jnp.float32)], axis=0
    )
    normed = (first * inverse_rms(first) * gain_ref[...]).astype(jnp.bfloat16)
    for span, weight_ref in spans(weight_refs):
        preact = lax.dot_general(
            normed,
            weight_ref[:, :half],
            (((1,), (1,)), ((), ())),
            preferred_element_type=jnp.float32,
        )
        normal_cdf = 0.5 * (1.0 + lax.erf(preact * root_half))
        density = jnp.exp(-0.5 * preact * preact) * inv_root_two_pi
        hidden_ref[:, span] = (preact * normal_cdf).astype(jnp.bfloat16)
        slopes_ref[:, span] = (normal_cdf + preact * density).astype(slopes_ref.dtype)
    branch = sum(
        jnp.dot(hidden_ref[:, span], weight_ref[:, half:], preferred_element_type=jnp.float32)
        for span, weight_ref in spans(weight_refs)
    )
    kept_ref[...] = branch[:tokens]
    sent_ref[...] = branch[tokens:].astype(sent_ref.dtype)


def acts_kernel(acts_ref, kept_ref, received_ref, acts_out_ref, first_out_ref):
    half = kept_ref.shape[1]
    branch = kept_ref[...] + received_ref[...].astype(jnp.float32)
    second = acts_ref[:, half:].astype(jnp.float32)
    new_first = ((second - branch) / coupling_scale).astype(jnp.bfloat16)
    acts_out_ref[:, :half] = new_first
    acts_out_ref[:, half:] = acts_ref[:, :half].astype(jnp.bfloat16)
    first_out_ref[...] = new_first


def backward_kernel(grads_ref, partner_ref, slopes_ref, *refs):
    weight_refs, (kept_ref, sent_ref, pre_grad) = refs[:-3], refs[-3:]
    tokens, half = partner_ref.shape
    cotangent = jnp.concatenate(
        [grads_ref[:, half:].astype(jnp.bfloat16), partner_ref[...].astype(jnp.bfloat16)], axis=0
    )
    for span, weight_ref in spans(weight_refs):
        hidden_grad = lax.dot_general(
            cotangent,
            weight_ref[:, half:],
            (((1,), (1,)), ((), ())),
            preferred_element_type=jnp.float32,
        )
        slopes = slopes_ref[:, span].astype(jnp.float32)
        pre_grad[:, span] = (hidden_grad * slopes).astype(jnp.bfloat16)
    norm_grad = sum(
        jnp.dot(pre_grad[:, span], weight_ref[:, :half], preferred_element_type=jnp.float32)
        for span, weight_ref in spans(weight_refs)
    )
    kept_ref[...] = norm_grad[:tokens]
    sent_ref[...] = norm_grad[tokens:].astype(sent_ref.dtype)


def grads_kernel(
    scale, acts_ref, grads_ref, gain_ref, kept_ref, received_ref, grads_out_ref, second_out_ref
):
    half = kept_ref.shape[1]
    first = acts_ref[:, :half].astype(jnp.float32)
    inv_rms = inverse_rms(first)
    scaled = (kept_ref[...] + received_ref[...].astype(jnp.float32)) * gain_ref[...]
    inner = jnp.mean(first * scaled, axis=-1, keepdims=True)
    input_grad = inv_rms * scaled - first * (inv_rms * inv_rms * inv_rms) * inner
    first_grad = grads_ref[:, :half].astype(jnp.float32)
    if scale != 1.0:
        first_grad = first_grad * scale
    new_second = (first_grad + input_grad).astype(jnp.bfloat16)
    grads_out_ref[:, :half] = grads_ref[:, half:].astype(jnp.bfloat16)
    grads_out_ref[:, half:] = new_second
    second_out_ref[...] = new_second


def outer_kernel(start, columns, *refs):
    ticks = len(refs) // 3
    hidden_refs, cotangent_refs, out_ref = refs[:ticks], refs[ticks:-1], refs[-1]
    count, half = out_ref.shape
    rows = jnp.concatenate([ref[:, start : start + count] for ref in hidden_refs], axis=0)
    cotangents = jnp.concatenate(
        [ref[:, at : at + half] for ref, at in zip(cotangent_refs, columns)], axis=0
    )
    total = lax.dot_general(
        rows, cotangents, (((0,), (0,)), ((), ())), preferred_element_type=jnp.float32
    )
    out_ref[...] = total.astype(out_ref.dtype)


def spans(weight_refs):
    offset = 0
    for ref in weight_refs:
        yield pl.ds(offset, ref.shape[0]), ref
        offset += ref.shape[0]


def in_vmem(count):
    return [pl.BlockSpec(memory_space=pltpu.VMEM)] * count


def cost(tokens, units, half):
    return pl.CostEstimate(
        flops=4 * tokens * units * half,
        bytes_accessed=4 * units * half + 4 * tokens * units,
        transcendentals=2 * tokens * units,
    )


def kernel_params():
    return pltpu.CompilerParams(vmem_limit_bytes=16 * 2**20)


def call(kernel, cost_estimate, outs, operands, scratch=()):
    return pl.pallas_call(
        kernel,
        out_shape=tuple(jax.ShapeDtypeStruct(shape, dtype) for shape, dtype in outs),
        in_specs=in_vmem(len(operands)),
        out_specs=tuple(in_vmem(len(outs))),
        scratch_shapes=list(scratch),
        cost_estimate=cost_estimate,
        compiler_params=kernel_params(),
    )(*operands)


def forward(acts, partner_first, gain, weights):
    tokens, half = partner_first.shape
    units = sum(w.shape[0] for w in weights)
    return call(
        forward_kernel,
        cost(2 * tokens, units, half),
        (
            ((2 * tokens, units), jnp.bfloat16),
            ((2 * tokens, units), jnp.bfloat16),
            ((tokens, half), jnp.float32),
            ((tokens, half), jnp.bfloat16),
        ),
        (acts, partner_first, gain, *weights),
    )


def backward(grads, partner_cotangent, slopes, weights):
    tokens, half = partner_cotangent.shape
    units = slopes.shape[1]
    return call(
        backward_kernel,
        cost(2 * tokens, units, half),
        (((tokens, half), jnp.float32), ((tokens, half), jnp.bfloat16)),
        (grads, partner_cotangent, slopes, *weights),
        (pltpu.VMEM((2 * tokens, units), jnp.bfloat16),),
    )


def small_cost(tokens, half):
    return pl.CostEstimate(
        flops=16 * tokens * half, bytes_accessed=16 * tokens * half, transcendentals=0
    )


def new_acts_of(acts, kept, received):
    tokens, half = kept.shape
    return call(
        acts_kernel,
        small_cost(tokens, half),
        (((tokens, 2 * half), jnp.bfloat16), ((tokens, half), jnp.bfloat16)),
        (acts, kept, received),
    )


def new_grads_of(scale, acts, grads, gain, kept, received):
    tokens, half = kept.shape
    return call(
        functools.partial(grads_kernel, scale),
        small_cost(tokens, half),
        (((tokens, 2 * half), jnp.bfloat16), ((tokens, half), jnp.bfloat16)),
        (acts, grads, gain, kept, received),
    )


def outer_rows(hiddens, cotangents, columns, start, count, half):
    tokens = hiddens[0].shape[0] * len(hiddens)
    return call(
        functools.partial(outer_kernel, start, columns),
        pl.CostEstimate(
            flops=2 * tokens * count * half,
            bytes_accessed=2 * (tokens * count + tokens * half + count * half),
            transcendentals=0,
        ),
        (((count, half), jnp.bfloat16),),
        (*hiddens, *cotangents),
    )[0]


def local(acts, grads, in_proj, out_proj, gain):
    half = acts.shape[2] // 2
    units = in_proj.shape[1]
    tick_count = min(4, lax.axis_size("section") // 2)
    shard = jnp.concatenate([in_proj[0], out_proj[0]], axis=1)
    group_size = len(alike_groups()[0])
    weights = gathered_along_x(exchanged(jnp.tile(shard, (group_size, 1))))
    quarter = group_size * units

    acts_pair, grads_pair, scale = acts[0], grads[0], 1.0
    partner_first = swapped_with_partner(acts_pair[:, :half])
    partner_cotangent = swapped_with_partner(grads_pair[:, half:].astype(jnp.bfloat16))
    hiddens, cotangents, columns = [], [], []
    for _ in range(tick_count - 1):
        hidden, slopes, kept, sent = forward(acts_pair, partner_first, gain, weights)
        received = swapped_with_partner(sent)
        hiddens.append(hidden)
        kept_grad, sent_grad = backward(grads_pair, partner_cotangent, slopes, weights)
        received_grad = swapped_with_partner(sent_grad)
        new_acts, new_first = new_acts_of(acts_pair, kept, received)
        next_acts = passed_back(new_acts)
        next_first = passed_back_to_partner(new_first)
        new_grads, new_second = new_grads_of(
            scale, acts_pair, grads_pair, gain, kept_grad, received_grad
        )
        next_grads = passed_back(new_grads)
        next_cotangent = passed_back_to_partner(new_second)
        cotangents += [new_grads, partner_cotangent]
        columns += [0, 0]
        acts_pair, grads_pair, scale = next_acts, next_grads, coupling_scale
        partner_first, partner_cotangent = next_first, next_cotangent

    hidden, slopes, kept, sent = forward(acts_pair, partner_first, gain, weights)
    hiddens.append(hidden)
    cotangents += [grads_pair, partner_cotangent]
    columns += [half, 0]
    outer = functools.partial(outer_rows, hiddens, cotangents, columns, count=quarter, half=half)
    parts = [outer(start=i * quarter) for i in (3, 1, 2)]
    from_far = swapped_along_x(parts[0], far_x)
    from_near = swapped_along_x(parts[1], near_x)
    from_next = swapped_along_x(parts[2], next_x)
    grads_pair, sent, _ = lax.optimization_barrier((grads_pair, sent, parts))
    kept_grad, sent_grad = backward(grads_pair, partner_cotangent, slopes, weights)
    received = swapped_with_partner(sent)
    received_grad = swapped_with_partner(sent_grad)
    own = outer(start=0)
    blocks = sum(x.astype(jnp.float32) for x in (own, from_near, from_next, from_far))
    blocks, received, received_grad = lax.optimization_barrier(
        (blocks.astype(jnp.bfloat16), received, received_grad)
    )
    new_acts, _ = new_acts_of(acts_pair, kept, received)
    new_grads, _ = new_grads_of(scale, acts_pair, grads_pair, gain, kept_grad, received_grad)
    parts = exchanged(blocks).reshape(-1, units, half)
    acts_pair, grads_pair = passed_back(new_acts), passed_back(new_grads)
    share = jnp.sum(parts.astype(jnp.float32), axis=0)

    grads_pair = grads_pair.astype(jnp.float32)
    grads_out = jnp.concatenate(
        [coupling_scale * grads_pair[:, :half], grads_pair[:, half:]], axis=1
    )
    return (acts_pair.astype(jnp.float32)[None], grads_out[None], share[None])


def solution(mesh):
    pair = P("section", "dp", None)
    return jax.shard_map(
        local,
        mesh=mesh,
        in_specs=(pair, pair, pair, pair, P("section", None)),
        out_specs=(pair, pair, pair),
        check_vma=False,
    )
```

```python
import functools

import jax
import jax.numpy as jnp
from jax import lax
from jax.experimental import pallas as pl
from jax.experimental.pallas import tpu as pltpu
from jax.sharding import PartitionSpec as P


coupling_scale = 32.0**0.25
rms_epsilon = 1e-06
root_half = 0.7071067811865476
inv_root_two_pi = 0.3989422804014327

x_size = 4
pair_size = 2


def dp_index(z, x, y):
    return (z * x_size + x) * pair_size + y


def z_size():
    return lax.axis_size("dp") // (x_size * pair_size)


def alike_groups():
    return [
        [
            dp_index(z, x, y)
            for z in range(parity, z_size(), 2)
            for y in range(pair_size)
        ]
        for parity in range(2)
        for x in range(x_size)
    ]


def swapped_along_x(block, peer):
    route = [
        (dp_index(z, peer(x), y), dp_index(z, x, y))
        for z in range(z_size())
        for x in range(x_size)
        for y in range(pair_size)
    ]
    return lax.ppermute(block, "dp", route)


def partner(index):
    return index ^ (x_size * pair_size)


def swapped_with_partner(block):
    return lax.ppermute(block, "dp", [(partner(i), i) for i in range(lax.axis_size("dp"))])


def near_x(x):
    return x ^ 1


def next_x(x):
    return (x + 1 if x % 2 else x - 1) % x_size


def far_x(x):
    return (x + 2) % x_size


def exchanged(blocks):
    return lax.all_to_all(
        blocks, "dp", 0, 0, axis_index_groups=alike_groups(), tiled=True
    )


def passed_back(block):
    devices = range(lax.axis_size("section"))
    return lax.ppermute(block, "section", [(i, i - 1) for i in devices if i])


def passed_back_to_partner(block):
    size = lax.axis_size("dp")
    route = [
        (section * size + i, (section - 1) * size + partner(i))
        for section in range(1, lax.axis_size("section"))
        for i in range(size)
    ]
    return lax.ppermute(block, ("section", "dp"), route)


def gathered_along_x(block):
    rows = block.shape[0] // 2
    near, following = swapped_along_x(block, near_x), swapped_along_x(block, next_x)
    far_head = swapped_along_x(following[:rows], near_x)
    far_tail = swapped_along_x(near[rows:], next_x)
    return block, near, following, far_head, far_tail


def inverse_rms(first):
    return lax.rsqrt(jnp.mean(first * first, axis=-1, keepdims=True) + rms_epsilon)


def pair_sums(straight, crossed):
    tokens = crossed.shape[0] // 2
    straight, crossed = straight.astype(jnp.float32), crossed.astype(jnp.float32)
    return jnp.concatenate(
        [straight[:tokens] + crossed[tokens:], straight[tokens:] + crossed[:tokens]], axis=0
    )


def pair_state(fresh, own_ref, other_ref, current):
    if fresh:
        half = other_ref.shape[1]
        waiting = half - current
        both = jnp.concatenate(
            [
                own_ref[:, current : current + half].astype(jnp.float32),
                other_ref[...].astype(jnp.float32),
            ],
            axis=0,
        )
        return both, own_ref[:, waiting : waiting + half]
    rows = other_ref.shape[0]
    return pair_sums(own_ref[:rows], other_ref[...]), own_ref[rows:].astype(jnp.float32)


def put_addends(last, straight_ref, crossed_ref, own, other, kept):
    tokens = own.shape[0]
    dtype = straight_ref.dtype
    straight_ref[:tokens] = own.astype(dtype)
    if last:
        crossed_ref[...] = other.astype(dtype)
        straight_ref[tokens:] = kept.astype(dtype)
    else:
        straight_ref[tokens : 2 * tokens] = other.astype(dtype)
        straight_ref[2 * tokens :] = kept.astype(dtype)
        crossed_ref[:tokens] = own.astype(dtype)
        crossed_ref[tokens:] = other.astype(dtype)


def forward_kernel(fresh, last, own_ref, other_ref, gain_ref, *refs):
    weight_refs, (hidden_ref, slopes_ref, straight_ref, crossed_ref) = refs[:-4], refs[-4:]
    first, second = pair_state(fresh, own_ref, other_ref, 0)
    tokens, half = second.shape
    normed = (first * inverse_rms(first) * gain_ref[...]).astype(jnp.bfloat16)
    for span, weight_ref in spans(weight_refs):
        preact = lax.dot_general(
            normed,
            weight_ref[:, :half],
            (((1,), (1,)), ((), ())),
            preferred_element_type=jnp.float32,
        )
        normal_cdf = 0.5 * (1.0 + lax.erf(preact * root_half))
        density = jnp.exp(-0.5 * preact * preact) * inv_root_two_pi
        hidden_ref[:, span] = (preact * normal_cdf).astype(jnp.bfloat16)
        slopes_ref[:, span] = (normal_cdf + preact * density).astype(slopes_ref.dtype)
    branch = sum(
        jnp.dot(hidden_ref[:, span], weight_ref[:, half:], preferred_element_type=jnp.float32)
        for span, weight_ref in spans(weight_refs)
    )
    own = (second - branch[:tokens]) / coupling_scale
    other = (0.0 - branch[tokens:]) / coupling_scale
    put_addends(last, straight_ref, crossed_ref, own, other, first[:tokens])


def backward_kernel(
    fresh, last, acts_ref, acts_other_ref, own_ref, other_ref, gain_ref, slopes_ref, *refs
):
    weight_refs, (cotangent_ref, straight_ref, crossed_ref, pre_grad) = refs[:-4], refs[-4:]
    half = gain_ref.shape[1]
    second_grad, first_grad = pair_state(fresh, own_ref, other_ref, half)
    tokens = first_grad.shape[0]
    if not fresh:
        first_grad = coupling_scale * first_grad
    cotangent = second_grad.astype(jnp.bfloat16)
    cotangent_ref[...] = cotangent
    for span, weight_ref in spans(weight_refs):
        hidden_grad = lax.dot_general(
            cotangent,
            weight_ref[:, half:],
            (((1,), (1,)), ((), ())),
            preferred_element_type=jnp.float32,
        )
        slopes = slopes_ref[:, span].astype(jnp.float32)
        pre_grad[:, span] = (hidden_grad * slopes).astype(jnp.bfloat16)
    norm_grad = sum(
        jnp.dot(pre_grad[:, span], weight_ref[:, :half], preferred_element_type=jnp.float32)
        for span, weight_ref in spans(weight_refs)
    )
    first, _ = pair_state(fresh, acts_ref, acts_other_ref, 0)
    inv_rms = inverse_rms(first)
    scaled = norm_grad * gain_ref[...]
    inner = jnp.mean(first * scaled, axis=-1, keepdims=True)
    input_grad = inv_rms * scaled - first * (inv_rms * inv_rms * inv_rms) * inner
    own = first_grad + input_grad[:tokens]
    put_addends(last, straight_ref, crossed_ref, own, input_grad[tokens:], cotangent[:tokens])


def cotangent_kernel(own_ref, other_ref, out_ref):
    rows = other_ref.shape[0]
    out_ref[...] = pair_sums(own_ref[:rows], other_ref[...]).astype(out_ref.dtype)


def output_kernel(kept_scale, kept_first, straight_ref, crossed_ref, out_ref):
    tokens, half = crossed_ref.shape
    fresh = straight_ref[:tokens].astype(jnp.float32) + crossed_ref[...].astype(jnp.float32)
    kept = straight_ref[tokens:].astype(jnp.float32)
    if kept_scale != 1.0:
        kept = kept * kept_scale
    first, second = (kept, fresh) if kept_first else (fresh, kept)
    out_ref[:, :half] = first
    out_ref[:, half:] = second


def outer_kernel(start, *refs):
    ticks = len(refs) // 2
    hidden_refs, cotangent_refs, out_ref = refs[:ticks], refs[ticks:-1], refs[-1]
    count = out_ref.shape[0]
    rows = jnp.concatenate([ref[:, start : start + count] for ref in hidden_refs], axis=0)
    cotangents = jnp.concatenate([ref[...] for ref in cotangent_refs], axis=0)
    total = lax.dot_general(
        rows, cotangents, (((0,), (0,)), ((), ())), preferred_element_type=jnp.float32
    )
    out_ref[...] = total.astype(out_ref.dtype)


def spans(weight_refs):
    offset = 0
    for ref in weight_refs:
        yield pl.ds(offset, ref.shape[0]), ref
        offset += ref.shape[0]


def in_vmem(count):
    return [pl.BlockSpec(memory_space=pltpu.VMEM)] * count


def cost(tokens, units, half):
    return pl.CostEstimate(
        flops=4 * tokens * units * half,
        bytes_accessed=4 * units * half + 4 * tokens * units,
        transcendentals=2 * tokens * units,
    )


def kernel_params():
    return pltpu.CompilerParams(vmem_limit_bytes=16 * 2**20)


def call(kernel, cost_estimate, outs, operands, scratch=()):
    return pl.pallas_call(
        kernel,
        out_shape=tuple(jax.ShapeDtypeStruct(shape, dtype) for shape, dtype in outs),
        in_specs=in_vmem(len(operands)),
        out_specs=tuple(in_vmem(len(outs))),
        scratch_shapes=list(scratch),
        cost_estimate=cost_estimate,
        compiler_params=kernel_params(),
    )(*operands)


def addend_shapes(last, tokens, half):
    straight, crossed = (2, 1) if last else (3, 2)
    return (
        ((straight * tokens, half), jnp.bfloat16),
        ((crossed * tokens, half), jnp.bfloat16),
    )


def forward(fresh, last, tokens, acts, gain, weights):
    half = gain.shape[1]
    units = sum(w.shape[0] for w in weights)
    return call(
        functools.partial(forward_kernel, fresh, last),
        cost(2 * tokens, units, half),
        (
            ((2 * tokens, units), jnp.bfloat16),
            ((2 * tokens, units), jnp.bfloat16),
            *addend_shapes(last, tokens, half),
        ),
        (*acts, gain, *weights),
    )


def backward(fresh, last, tokens, acts, grads, gain, slopes, weights):
    half = gain.shape[1]
    units = slopes.shape[1]
    return call(
        functools.partial(backward_kernel, fresh, last),
        cost(2 * tokens, units, half),
        (((2 * tokens, half), jnp.bfloat16), *addend_shapes(last, tokens, half)),
        (*acts, *grads, gain, slopes, *weights),
        (pltpu.VMEM((2 * tokens, units), jnp.bfloat16),),
    )


def small_cost(tokens, half):
    return pl.CostEstimate(
        flops=16 * tokens * half, bytes_accessed=16 * tokens * half, transcendentals=0
    )


def cotangent_of(grads):
    _, crossed = grads
    return call(
        cotangent_kernel, small_cost(*crossed.shape), ((crossed.shape, jnp.bfloat16),), grads
    )[0]


def output_of(kept_scale, kept_first, straight, crossed):
    tokens, half = crossed.shape
    return call(
        functools.partial(output_kernel, kept_scale, kept_first),
        small_cost(tokens, half),
        (((tokens, 2 * half), jnp.float32),),
        (straight, crossed),
    )[0]


def outer_rows(hiddens, cotangents, start, count):
    half = cotangents[0].shape[1]
    tokens = hiddens[0].shape[0] * len(hiddens)
    return call(
        functools.partial(outer_kernel, start),
        pl.CostEstimate(
            flops=2 * tokens * count * half,
            bytes_accessed=2 * (tokens * count + tokens * half + count * half),
            transcendentals=0,
        ),
        (((count, half), jnp.bfloat16),),
        (*hiddens, *cotangents),
    )[0]


def sent_back(straight, crossed):
    crossed = passed_back_to_partner(crossed)
    straight = passed_back(straight)
    return straight, crossed


def local(acts, grads, in_proj, out_proj, gain):
    tokens, half = acts.shape[1], acts.shape[2] // 2
    units = in_proj.shape[1]
    tick_count = min(4, lax.axis_size("section") // 2)
    shard = jnp.concatenate([in_proj[0], out_proj[0]], axis=1)
    group_size = len(alike_groups()[0])
    weights = gathered_along_x(exchanged(jnp.tile(shard, (group_size, 1))))
    quarter = group_size * units

    acts_pair = (acts[0], swapped_with_partner(acts[0, :, :half]))
    grads_pair = (grads[0], swapped_with_partner(grads[0, :, half:].astype(jnp.bfloat16)))
    hiddens, cotangents = [], []
    for tick_index in range(tick_count):
        fresh, last = tick_index == 0, tick_index == tick_count - 1
        hidden, slopes, *addends = forward(fresh, last, tokens, acts_pair, gain, weights)
        hiddens.append(hidden)
        next_acts = sent_back(*addends)
        if last:
            grads_pair, hidden, addends = lax.optimization_barrier((grads_pair, hidden, addends))
            cotangents.append(cotangent_of(grads_pair))
            outer = functools.partial(outer_rows, hiddens, cotangents, count=quarter)
            parts = [outer(i * quarter) for i in (3, 1, 2)]
            from_far = swapped_along_x(parts[0], far_x)
            from_near = swapped_along_x(parts[1], near_x)
            from_next = swapped_along_x(parts[2], next_x)
            slopes, _ = lax.optimization_barrier((slopes, parts))
        cotangent, *addends = backward(
            fresh, last, tokens, acts_pair, grads_pair, gain, slopes, weights
        )
        if last:
            own = outer(0)
            blocks = sum(
                x.astype(jnp.float32) for x in (own, from_near, from_next, from_far)
            ).astype(jnp.bfloat16)
            parts = exchanged(blocks).reshape(-1, units, half)
        else:
            cotangents.append(cotangent)
        next_grads = sent_back(*addends)
        acts_pair, grads_pair = next_acts, next_grads

    share = jnp.sum(parts.astype(jnp.float32), axis=0)
    acts_out = output_of(1.0, False, *acts_pair)
    grads_out = output_of(coupling_scale, True, *grads_pair)
    return (acts_out[None], grads_out[None], share[None])


def solution(mesh):
    pair = P("section", "dp", None)
    return jax.shard_map(
        local,
        mesh=mesh,
        in_specs=(pair, pair, pair, pair, P("section", None)),
        out_specs=(pair, pair, pair),
        check_vma=False,
    )
```

```python
import functools

import jax
import jax.numpy as jnp
from jax import lax
from jax.experimental import pallas as pl
from jax.experimental.pallas import tpu as pltpu
from jax.sharding import PartitionSpec as P


coupling_scale = 32.0**0.25
rms_epsilon = 1e-06
root_half = 0.7071067811865476
inv_root_two_pi = 0.3989422804014327

x_size = 4
pair_size = 2


def dp_index(z, x, y):
    return (z * x_size + x) * pair_size + y


def z_size():
    return lax.axis_size("dp") // (x_size * pair_size)


def alike_groups():
    return [
        [
            dp_index(z, x, y)
            for z in range(parity, z_size(), 2)
            for y in range(pair_size)
        ]
        for parity in range(2)
        for x in range(x_size)
    ]


def swapped_along_x(block, peer):
    route = [
        (dp_index(z, peer(x), y), dp_index(z, x, y))
        for z in range(z_size())
        for x in range(x_size)
        for y in range(pair_size)
    ]
    return lax.ppermute(block, "dp", route)


def partner(index):
    return index ^ (x_size * pair_size)


def swapped_with_partner(block):
    return lax.ppermute(block, "dp", [(partner(i), i) for i in range(lax.axis_size("dp"))])


def near_x(x):
    return x ^ 1


def next_x(x):
    return (x + 1 if x % 2 else x - 1) % x_size


def far_x(x):
    return (x + 2) % x_size


def exchanged(blocks):
    return lax.all_to_all(
        blocks, "dp", 0, 0, axis_index_groups=alike_groups(), tiled=True
    )


def passed_back(block):
    devices = range(lax.axis_size("section"))
    return lax.ppermute(block, "section", [(i, i - 1) for i in devices if i])


def passed_back_to_partner(block):
    size = lax.axis_size("dp")
    route = [
        (section * size + i, (section - 1) * size + partner(i))
        for section in range(1, lax.axis_size("section"))
        for i in range(size)
    ]
    return lax.ppermute(block, ("section", "dp"), route)


def gathered_along_x(block):
    rows = block.shape[0] // 2
    near, following = swapped_along_x(block, near_x), swapped_along_x(block, next_x)
    far_head = swapped_along_x(following[:rows], near_x)
    far_tail = swapped_along_x(near[rows:], next_x)
    return block, near, following, far_head, far_tail


def inverse_rms(first):
    return lax.rsqrt(jnp.mean(first * first, axis=-1, keepdims=True) + rms_epsilon)


def pair_sums(straight, crossed):
    tokens = crossed.shape[0] // 2
    straight, crossed = straight.astype(jnp.float32), crossed.astype(jnp.float32)
    return jnp.concatenate(
        [straight[:tokens] + crossed[tokens:], straight[tokens:] + crossed[:tokens]], axis=0
    )


def pair_state(fresh, own_ref, other_ref, current):
    if fresh:
        half = other_ref.shape[1]
        waiting = half - current
        both = jnp.concatenate(
            [
                own_ref[:, current : current + half].astype(jnp.float32),
                other_ref[...].astype(jnp.float32),
            ],
            axis=0,
        )
        return both, own_ref[:, waiting : waiting + half]
    rows = other_ref.shape[0]
    return pair_sums(own_ref[:rows], other_ref[...]), own_ref[rows:].astype(jnp.float32)


def put_addends(last, straight_ref, crossed_ref, own, other, kept):
    tokens = own.shape[0]
    dtype = straight_ref.dtype
    straight_ref[:tokens] = own.astype(dtype)
    if last:
        crossed_ref[...] = other.astype(dtype)
        straight_ref[tokens:] = kept.astype(dtype)
    else:
        straight_ref[tokens : 2 * tokens] = other.astype(dtype)
        straight_ref[2 * tokens :] = kept.astype(dtype)
        crossed_ref[:tokens] = own.astype(dtype)
        crossed_ref[tokens:] = other.astype(dtype)


def forward_kernel(fresh, last, own_ref, other_ref, gain_ref, *refs):
    weight_refs, (hidden_ref, slopes_ref, straight_ref, crossed_ref) = refs[:-4], refs[-4:]
    first, second = pair_state(fresh, own_ref, other_ref, 0)
    tokens, half = second.shape
    normed = (first * inverse_rms(first) * gain_ref[...]).astype(jnp.bfloat16)
    for span, weight_ref in spans(weight_refs):
        preact = lax.dot_general(
            normed,
            weight_ref[:, :half],
            (((1,), (1,)), ((), ())),
            preferred_element_type=jnp.float32,
        )
        normal_cdf = 0.5 * (1.0 + lax.erf(preact * root_half))
        density = jnp.exp(-0.5 * preact * preact) * inv_root_two_pi
        hidden_ref[:, span] = (preact * normal_cdf).astype(jnp.bfloat16)
        slopes_ref[:, span] = (normal_cdf + preact * density).astype(slopes_ref.dtype)
    branch = sum(
        jnp.dot(hidden_ref[:, span], weight_ref[:, half:], preferred_element_type=jnp.float32)
        for span, weight_ref in spans(weight_refs)
    )
    own = (second - branch[:tokens]) / coupling_scale
    other = (0.0 - branch[tokens:]) / coupling_scale
    put_addends(last, straight_ref, crossed_ref, own, other, first[:tokens])


def backward_kernel(
    fresh, last, acts_ref, acts_other_ref, own_ref, other_ref, gain_ref, slopes_ref, *refs
):
    weight_refs, (cotangent_ref, straight_ref, crossed_ref, pre_grad) = refs[:-4], refs[-4:]
    half = gain_ref.shape[1]
    second_grad, first_grad = pair_state(fresh, own_ref, other_ref, half)
    tokens = first_grad.shape[0]
    if not fresh:
        first_grad = coupling_scale * first_grad
    cotangent = second_grad.astype(jnp.bfloat16)
    cotangent_ref[...] = cotangent
    for span, weight_ref in spans(weight_refs):
        hidden_grad = lax.dot_general(
            cotangent,
            weight_ref[:, half:],
            (((1,), (1,)), ((), ())),
            preferred_element_type=jnp.float32,
        )
        slopes = slopes_ref[:, span].astype(jnp.float32)
        pre_grad[:, span] = (hidden_grad * slopes).astype(jnp.bfloat16)
    norm_grad = sum(
        jnp.dot(pre_grad[:, span], weight_ref[:, :half], preferred_element_type=jnp.float32)
        for span, weight_ref in spans(weight_refs)
    )
    first, _ = pair_state(fresh, acts_ref, acts_other_ref, 0)
    inv_rms = inverse_rms(first)
    scaled = norm_grad * gain_ref[...]
    inner = jnp.mean(first * scaled, axis=-1, keepdims=True)
    input_grad = inv_rms * scaled - first * (inv_rms * inv_rms * inv_rms) * inner
    own = first_grad + input_grad[:tokens]
    put_addends(last, straight_ref, crossed_ref, own, input_grad[tokens:], cotangent[:tokens])


def cotangent_kernel(own_ref, other_ref, out_ref):
    rows = other_ref.shape[0]
    out_ref[...] = pair_sums(own_ref[:rows], other_ref[...]).astype(out_ref.dtype)


def output_kernel(kept_scale, kept_first, straight_ref, crossed_ref, out_ref):
    tokens, half = crossed_ref.shape
    fresh = straight_ref[:tokens].astype(jnp.float32) + crossed_ref[...].astype(jnp.float32)
    kept = straight_ref[tokens:].astype(jnp.float32)
    if kept_scale != 1.0:
        kept = kept * kept_scale
    first, second = (kept, fresh) if kept_first else (fresh, kept)
    out_ref[:, :half] = first
    out_ref[:, half:] = second


def outer_kernel(start, *refs):
    ticks = len(refs) // 2
    hidden_refs, cotangent_refs, out_ref = refs[:ticks], refs[ticks:-1], refs[-1]
    count = out_ref.shape[0]
    rows = jnp.concatenate([ref[:, start : start + count] for ref in hidden_refs], axis=0)
    cotangents = jnp.concatenate([ref[...] for ref in cotangent_refs], axis=0)
    total = lax.dot_general(
        rows, cotangents, (((0,), (0,)), ((), ())), preferred_element_type=jnp.float32
    )
    out_ref[...] = total.astype(out_ref.dtype)


def spans(weight_refs):
    offset = 0
    for ref in weight_refs:
        yield pl.ds(offset, ref.shape[0]), ref
        offset += ref.shape[0]


def in_vmem(count):
    return [pl.BlockSpec(memory_space=pltpu.VMEM)] * count


def cost(tokens, units, half):
    return pl.CostEstimate(
        flops=4 * tokens * units * half,
        bytes_accessed=4 * units * half + 4 * tokens * units,
        transcendentals=2 * tokens * units,
    )


def kernel_params():
    return pltpu.CompilerParams(vmem_limit_bytes=16 * 2**20)


def call(kernel, cost_estimate, outs, operands, scratch=()):
    return pl.pallas_call(
        kernel,
        out_shape=tuple(jax.ShapeDtypeStruct(shape, dtype) for shape, dtype in outs),
        in_specs=in_vmem(len(operands)),
        out_specs=tuple(in_vmem(len(outs))),
        scratch_shapes=list(scratch),
        cost_estimate=cost_estimate,
        compiler_params=kernel_params(),
    )(*operands)


def addend_shapes(last, tokens, half):
    straight, crossed = (2, 1) if last else (3, 2)
    return (
        ((straight * tokens, half), jnp.bfloat16),
        ((crossed * tokens, half), jnp.bfloat16),
    )


def forward(fresh, last, tokens, acts, gain, weights):
    half = gain.shape[1]
    units = sum(w.shape[0] for w in weights)
    return call(
        functools.partial(forward_kernel, fresh, last),
        cost(2 * tokens, units, half),
        (
            ((2 * tokens, units), jnp.bfloat16),
            ((2 * tokens, units), jnp.bfloat16),
            *addend_shapes(last, tokens, half),
        ),
        (*acts, gain, *weights),
    )


def backward(fresh, last, tokens, acts, grads, gain, slopes, weights):
    half = gain.shape[1]
    units = slopes.shape[1]
    return call(
        functools.partial(backward_kernel, fresh, last),
        cost(2 * tokens, units, half),
        (((2 * tokens, half), jnp.bfloat16), *addend_shapes(last, tokens, half)),
        (*acts, *grads, gain, slopes, *weights),
        (pltpu.VMEM((2 * tokens, units), jnp.bfloat16),),
    )


def small_cost(tokens, half):
    return pl.CostEstimate(
        flops=16 * tokens * half, bytes_accessed=16 * tokens * half, transcendentals=0
    )


def cotangent_of(grads):
    _, crossed = grads
    return call(
        cotangent_kernel, small_cost(*crossed.shape), ((crossed.shape, jnp.bfloat16),), grads
    )[0]


def output_of(kept_scale, kept_first, straight, crossed):
    tokens, half = crossed.shape
    return call(
        functools.partial(output_kernel, kept_scale, kept_first),
        small_cost(tokens, half),
        (((tokens, 2 * half), jnp.float32),),
        (straight, crossed),
    )[0]


def outer_rows(hiddens, cotangents, start, count):
    half = cotangents[0].shape[1]
    tokens = hiddens[0].shape[0] * len(hiddens)
    return call(
        functools.partial(outer_kernel, start),
        pl.CostEstimate(
            flops=2 * tokens * count * half,
            bytes_accessed=2 * (tokens * count + tokens * half + count * half),
            transcendentals=0,
        ),
        (((count, half), jnp.bfloat16),),
        (*hiddens, *cotangents),
    )[0]


def sent_back(straight, crossed):
    crossed = passed_back_to_partner(crossed)
    straight = passed_back(straight)
    return straight, crossed


def local(acts, grads, in_proj, out_proj, gain):
    tokens, half = acts.shape[1], acts.shape[2] // 2
    units = in_proj.shape[1]
    tick_count = min(4, lax.axis_size("section") // 2)
    shard = jnp.concatenate([in_proj[0], out_proj[0]], axis=1)
    group_size = len(alike_groups()[0])
    weights = gathered_along_x(exchanged(jnp.tile(shard, (group_size, 1))))
    quarter = group_size * units

    acts_pair = (acts[0], swapped_with_partner(acts[0, :, :half]))
    grads_pair = (grads[0], swapped_with_partner(grads[0, :, half:].astype(jnp.bfloat16)))
    hiddens, cotangents = [], []
    for tick_index in range(tick_count):
        fresh, last = tick_index == 0, tick_index == tick_count - 1
        hidden, slopes, *addends = forward(fresh, last, tokens, acts_pair, gain, weights)
        hiddens.append(hidden)
        next_acts = sent_back(*addends)
        if last:
            grads_pair, hidden, addends = lax.optimization_barrier((grads_pair, hidden, addends))
            cotangents.append(cotangent_of(grads_pair))
            outer = functools.partial(outer_rows, hiddens, cotangents, count=quarter)
            far_rows = outer(3 * quarter)
            near_rows = outer(quarter)
            next_rows = outer(2 * quarter)
            from_far = swapped_along_x(far_rows, far_x)
            from_near = swapped_along_x(near_rows, near_x)
            from_next = swapped_along_x(next_rows, next_x)
            slopes, _ = lax.optimization_barrier((slopes, (far_rows, near_rows, next_rows)))
        cotangent, *addends = backward(
            fresh, last, tokens, acts_pair, grads_pair, gain, slopes, weights
        )
        if last:
            own = outer(0)
            blocks = sum(
                x.astype(jnp.float32) for x in (own, from_near, from_next, from_far)
            ).astype(jnp.bfloat16)
            blocks, addends = lax.optimization_barrier((blocks, addends))
            parts = exchanged(blocks).reshape(-1, units, half)
        else:
            cotangents.append(cotangent)
        next_grads = sent_back(*addends)
        acts_pair, grads_pair = next_acts, next_grads

    share = jnp.sum(parts.astype(jnp.float32), axis=0)
    acts_out = output_of(1.0, False, *acts_pair)
    grads_out = output_of(coupling_scale, True, *grads_pair)
    return (acts_out[None], grads_out[None], share[None])


def solution(mesh):
    pair = P("section", "dp", None)
    return jax.shard_map(
        local,
        mesh=mesh,
        in_specs=(pair, pair, pair, pair, P("section", None)),
        out_specs=(pair, pair, pair),
        check_vma=False,
    )
```

```python
import functools

import jax
import jax.numpy as jnp
from jax import lax
from jax.experimental import pallas as pl
from jax.experimental.pallas import tpu as pltpu
from jax.sharding import PartitionSpec as P


coupling_scale = 32.0**0.25
rms_epsilon = 1e-06
root_half = 0.7071067811865476
inv_root_two_pi = 0.3989422804014327

x_size = 4
pair_size = 2
chunk = 256


def dp_index(z, x, y):
    return (z * x_size + x) * pair_size + y


def z_size():
    return lax.axis_size("dp") // (x_size * pair_size)


def alike_groups():
    return [
        [
            dp_index(z, x, y)
            for x in range(x_size)
            for z in range(parity, z_size(), 2)
            for y in range(pair_size)
        ]
        for parity in range(2)
    ]


def partner(index):
    return index ^ (x_size * pair_size)


def swapped_with_partner(block):
    return lax.ppermute(block, "dp", [(partner(i), i) for i in range(lax.axis_size("dp"))])


def exchanged(blocks):
    return lax.all_to_all(
        blocks, "dp", 0, 0, axis_index_groups=alike_groups(), tiled=True
    )


def passed_back(block):
    devices = range(lax.axis_size("section"))
    return lax.ppermute(block, "section", [(i, i - 1) for i in devices if i])


def passed_back_to_partner(block):
    size = lax.axis_size("dp")
    route = [
        (section * size + i, (section - 1) * size + partner(i))
        for section in range(1, lax.axis_size("section"))
        for i in range(size)
    ]
    return lax.ppermute(block, ("section", "dp"), route)


def inverse_rms(first):
    return lax.rsqrt(jnp.mean(first * first, axis=-1, keepdims=True) + rms_epsilon)


def pair_sums(straight, crossed):
    tokens = crossed.shape[0] // 2
    straight, crossed = straight.astype(jnp.float32), crossed.astype(jnp.float32)
    return jnp.concatenate(
        [straight[:tokens] + crossed[tokens:], straight[tokens:] + crossed[:tokens]], axis=0
    )


def pair_state(fresh, own_ref, other_ref, current):
    if fresh:
        half = other_ref.shape[1]
        waiting = half - current
        both = jnp.concatenate(
            [
                own_ref[:, current : current + half].astype(jnp.float32),
                other_ref[...].astype(jnp.float32),
            ],
            axis=0,
        )
        return both, own_ref[:, waiting : waiting + half]
    rows = other_ref.shape[0]
    return pair_sums(own_ref[:rows], other_ref[...]), own_ref[rows:].astype(jnp.float32)


def put_addends(last, straight_ref, crossed_ref, own, other, kept):
    tokens = own.shape[0]
    dtype = straight_ref.dtype
    straight_ref[:tokens] = own.astype(dtype)
    if last:
        crossed_ref[...] = other.astype(dtype)
        straight_ref[tokens:] = kept.astype(dtype)
    else:
        straight_ref[tokens : 2 * tokens] = other.astype(dtype)
        straight_ref[2 * tokens :] = kept.astype(dtype)
        crossed_ref[:tokens] = own.astype(dtype)
        crossed_ref[tokens:] = other.astype(dtype)


def forward_kernel(fresh, last, own_ref, other_ref, gain_ref, weight_ref, *refs):
    hidden_ref, slopes_ref, straight_ref, crossed_ref = refs
    first, second = pair_state(fresh, own_ref, other_ref, 0)
    tokens, half = second.shape
    normed = (first * inverse_rms(first) * gain_ref[...]).astype(jnp.bfloat16)
    for span, part_ref in spans(weight_ref):
        preact = lax.dot_general(
            normed,
            part_ref[:, :half],
            (((1,), (1,)), ((), ())),
            preferred_element_type=jnp.float32,
        )
        normal_cdf = 0.5 * (1.0 + lax.erf(preact * root_half))
        density = jnp.exp(-0.5 * preact * preact) * inv_root_two_pi
        hidden_ref[:, span] = (preact * normal_cdf).astype(jnp.bfloat16)
        slopes_ref[:, span] = (normal_cdf + preact * density).astype(slopes_ref.dtype)
    branch = sum(
        jnp.dot(hidden_ref[:, span], part_ref[:, half:], preferred_element_type=jnp.float32)
        for span, part_ref in spans(weight_ref)
    )
    own = (second - branch[:tokens]) / coupling_scale
    other = (0.0 - branch[tokens:]) / coupling_scale
    put_addends(last, straight_ref, crossed_ref, own, other, first[:tokens])


def backward_kernel(
    fresh, last, acts_ref, acts_other_ref, own_ref, other_ref, gain_ref, slopes_ref, weight_ref, *refs
):
    cotangent_ref, straight_ref, crossed_ref, pre_grad = refs
    half = gain_ref.shape[1]
    second_grad, first_grad = pair_state(fresh, own_ref, other_ref, half)
    tokens = first_grad.shape[0]
    if not fresh:
        first_grad = coupling_scale * first_grad
    cotangent = second_grad.astype(jnp.bfloat16)
    cotangent_ref[...] = cotangent
    for span, part_ref in spans(weight_ref):
        hidden_grad = lax.dot_general(
            cotangent,
            part_ref[:, half:],
            (((1,), (1,)), ((), ())),
            preferred_element_type=jnp.float32,
        )
        slopes = slopes_ref[:, span].astype(jnp.float32)
        pre_grad[:, span] = (hidden_grad * slopes).astype(jnp.bfloat16)
    norm_grad = sum(
        jnp.dot(pre_grad[:, span], part_ref[:, :half], preferred_element_type=jnp.float32)
        for span, part_ref in spans(weight_ref)
    )
    first, _ = pair_state(fresh, acts_ref, acts_other_ref, 0)
    inv_rms = inverse_rms(first)
    scaled = norm_grad * gain_ref[...]
    inner = jnp.mean(first * scaled, axis=-1, keepdims=True)
    input_grad = inv_rms * scaled - first * (inv_rms * inv_rms * inv_rms) * inner
    own = first_grad + input_grad[:tokens]
    put_addends(last, straight_ref, crossed_ref, own, input_grad[tokens:], cotangent[:tokens])


def cotangent_kernel(own_ref, other_ref, out_ref):
    rows = other_ref.shape[0]
    out_ref[...] = pair_sums(own_ref[:rows], other_ref[...]).astype(out_ref.dtype)


def output_kernel(kept_scale, kept_first, straight_ref, crossed_ref, out_ref):
    tokens, half = crossed_ref.shape
    fresh = straight_ref[:tokens].astype(jnp.float32) + crossed_ref[...].astype(jnp.float32)
    kept = straight_ref[tokens:].astype(jnp.float32)
    if kept_scale != 1.0:
        kept = kept * kept_scale
    first, second = (kept, fresh) if kept_first else (fresh, kept)
    out_ref[:, :half] = first
    out_ref[:, half:] = second


def outer_kernel(*refs):
    ticks = len(refs) // 2
    hidden_refs, cotangent_refs, out_ref = refs[:ticks], refs[ticks:-1], refs[-1]
    cotangents = jnp.concatenate([ref[...] for ref in cotangent_refs], axis=0)
    for start in range(0, out_ref.shape[0], chunk):
        rows = jnp.concatenate([ref[:, start : start + chunk] for ref in hidden_refs], axis=0)
        total = lax.dot_general(
            rows, cotangents, (((0,), (0,)), ((), ())), preferred_element_type=jnp.float32
        )
        out_ref[start : start + chunk] = total.astype(out_ref.dtype)


def spans(weight_ref):
    for start in range(0, weight_ref.shape[0], chunk):
        yield pl.ds(start, chunk), weight_ref.at[pl.ds(start, chunk)]


def in_vmem(count):
    return [pl.BlockSpec(memory_space=pltpu.VMEM)] * count


def cost(tokens, units, half):
    return pl.CostEstimate(
        flops=4 * tokens * units * half,
        bytes_accessed=4 * units * half + 4 * tokens * units,
        transcendentals=2 * tokens * units,
    )


def kernel_params():
    return pltpu.CompilerParams(vmem_limit_bytes=16 * 2**20)


def call(kernel, cost_estimate, outs, operands, scratch=()):
    return pl.pallas_call(
        kernel,
        out_shape=tuple(jax.ShapeDtypeStruct(shape, dtype) for shape, dtype in outs),
        in_specs=in_vmem(len(operands)),
        out_specs=tuple(in_vmem(len(outs))),
        scratch_shapes=list(scratch),
        cost_estimate=cost_estimate,
        compiler_params=kernel_params(),
    )(*operands)


def addend_shapes(last, tokens, half):
    straight, crossed = (2, 1) if last else (3, 2)
    return (
        ((straight * tokens, half), jnp.bfloat16),
        ((crossed * tokens, half), jnp.bfloat16),
    )


def forward(fresh, last, tokens, acts, gain, weights):
    half = gain.shape[1]
    units = weights.shape[0]
    return call(
        functools.partial(forward_kernel, fresh, last),
        cost(2 * tokens, units, half),
        (
            ((2 * tokens, units), jnp.bfloat16),
            ((2 * tokens, units), jnp.bfloat16),
            *addend_shapes(last, tokens, half),
        ),
        (*acts, gain, weights),
    )


def backward(fresh, last, tokens, acts, grads, gain, slopes, weights):
    half = gain.shape[1]
    units = slopes.shape[1]
    return call(
        functools.partial(backward_kernel, fresh, last),
        cost(2 * tokens, units, half),
        (((2 * tokens, half), jnp.bfloat16), *addend_shapes(last, tokens, half)),
        (*acts, *grads, gain, slopes, weights),
        (pltpu.VMEM((2 * tokens, units), jnp.bfloat16),),
    )


def small_cost(tokens, half):
    return pl.CostEstimate(
        flops=16 * tokens * half, bytes_accessed=16 * tokens * half, transcendentals=0
    )


def cotangent_of(grads):
    _, crossed = grads
    return call(
        cotangent_kernel, small_cost(*crossed.shape), ((crossed.shape, jnp.bfloat16),), grads
    )[0]


def output_of(kept_scale, kept_first, straight, crossed):
    tokens, half = crossed.shape
    return call(
        functools.partial(output_kernel, kept_scale, kept_first),
        small_cost(tokens, half),
        (((tokens, 2 * half), jnp.float32),),
        (straight, crossed),
    )[0]


def outer_product(hiddens, cotangents):
    half = cotangents[0].shape[1]
    tokens, units = hiddens[0].shape
    return call(
        outer_kernel,
        cost(len(hiddens) * tokens, units, half // 2),
        (((units, half), jnp.bfloat16),),
        (*hiddens, *cotangents),
    )[0]


def sent_back(straight, crossed):
    crossed = passed_back_to_partner(crossed)
    straight = passed_back(straight)
    return straight, crossed


def local(acts, grads, in_proj, out_proj, gain):
    tokens, half = acts.shape[1], acts.shape[2] // 2
    units = in_proj.shape[1]
    tick_count = min(4, lax.axis_size("section") // 2)
    shard = jnp.concatenate([in_proj[0], out_proj[0]], axis=1)
    group_size = len(alike_groups()[0])
    weights = exchanged(jnp.tile(shard, (group_size, 1)))

    acts_pair = (acts[0], swapped_with_partner(acts[0, :, :half]))
    grads_pair = (grads[0], swapped_with_partner(grads[0, :, half:].astype(jnp.bfloat16)))
    hiddens, cotangents = [], []
    for tick_index in range(tick_count):
        fresh, last = tick_index == 0, tick_index == tick_count - 1
        hidden, slopes, *addends = forward(fresh, last, tokens, acts_pair, gain, weights)
        hiddens.append(hidden)
        next_acts = sent_back(*addends)
        if last:
            grads_pair, hidden, addends = lax.optimization_barrier((grads_pair, hidden, addends))
            cotangents.append(cotangent_of(grads_pair))
            blocks = outer_product(hiddens, cotangents)
            parts = exchanged(blocks).reshape(-1, units, half)
        cotangent, *addends = backward(
            fresh, last, tokens, acts_pair, grads_pair, gain, slopes, weights
        )
        if not last:
            cotangents.append(cotangent)
        next_grads = sent_back(*addends)
        acts_pair, grads_pair = next_acts, next_grads

    share = jnp.sum(parts.astype(jnp.float32), axis=0)
    acts_out = output_of(1.0, False, *acts_pair)
    grads_out = output_of(coupling_scale, True, *grads_pair)
    return (acts_out[None], grads_out[None], share[None])


def solution(mesh):
    pair = P("section", "dp", None)
    return jax.shard_map(
        local,
        mesh=mesh,
        in_specs=(pair, pair, pair, pair, P("section", None)),
        out_specs=(pair, pair, pair),
        check_vma=False,
    )
```

```python
import functools

import jax
import jax.numpy as jnp
from jax import lax
from jax.experimental import pallas as pl
from jax.experimental.pallas import tpu as pltpu
from jax.sharding import PartitionSpec as P


coupling_scale = 32.0**0.25
rms_epsilon = 1e-06
root_half = 0.7071067811865476
inv_root_two_pi = 0.3989422804014327

x_size = 4
pair_size = 2


def dp_index(z, x, y):
    return (z * x_size + x) * pair_size + y


def z_size():
    return lax.axis_size("dp") // (x_size * pair_size)


def alike_groups():
    return [
        [
            dp_index(z, x, y)
            for z in range(parity, z_size(), 2)
            for y in range(pair_size)
        ]
        for parity in range(2)
        for x in range(x_size)
    ]


def swapped_along_x(block, peer):
    route = [
        (dp_index(z, peer(x), y), dp_index(z, x, y))
        for z in range(z_size())
        for x in range(x_size)
        for y in range(pair_size)
    ]
    return lax.ppermute(block, "dp", route)


def partner(index):
    return index ^ (x_size * pair_size)


def swapped_with_partner(block):
    return lax.ppermute(block, "dp", [(partner(i), i) for i in range(lax.axis_size("dp"))])


def near_x(x):
    return x ^ 1


def next_x(x):
    return (x + 1 if x % 2 else x - 1) % x_size


def far_x(x):
    return (x + 2) % x_size


def exchanged(blocks):
    return lax.all_to_all(
        blocks, "dp", 0, 0, axis_index_groups=alike_groups(), tiled=True
    )


def passed_back(block):
    devices = range(lax.axis_size("section"))
    return lax.ppermute(block, "section", [(i, i - 1) for i in devices if i])


def passed_back_to_partner(block):
    size = lax.axis_size("dp")
    route = [
        (section * size + i, (section - 1) * size + partner(i))
        for section in range(1, lax.axis_size("section"))
        for i in range(size)
    ]
    return lax.ppermute(block, ("section", "dp"), route)


def gathered_along_x(block):
    rows = block.shape[0] // 2
    near, following = swapped_along_x(block, near_x), swapped_along_x(block, next_x)
    far_head = swapped_along_x(following[:rows], near_x)
    far_tail = swapped_along_x(near[rows:], next_x)
    return block, near, following, far_head, far_tail


def inverse_rms(first):
    return lax.rsqrt(jnp.mean(first * first, axis=-1, keepdims=True) + rms_epsilon)


def split(counts, refs):
    parts, start = [], 0
    for count in counts:
        parts.append(refs[start : start + count])
        start += count
    return *parts, refs[start:]


def pair_sums(straight, crossed):
    tokens = crossed.shape[0] // 2
    straight, crossed = straight.astype(jnp.float32), crossed.astype(jnp.float32)
    return jnp.concatenate(
        [straight[:tokens] + crossed[tokens:], straight[tokens:] + crossed[:tokens]], axis=0
    )


def pair_state(fresh, current, waiting_at, state_refs):
    own_ref, other_ref = state_refs[:2]
    if fresh:
        _, half = other_ref.shape
        waiting = half - current
        both = jnp.concatenate(
            [
                own_ref[:, current : current + half].astype(jnp.float32),
                other_ref[...].astype(jnp.float32),
            ],
            axis=0,
        )
        return both, own_ref[:, waiting : waiting + half]
    rows = other_ref.shape[0]
    both = pair_sums(own_ref[:rows], other_ref[...])
    if waiting_at is None:
        return both, None
    if len(state_refs) == 3:
        start = waiting_at * (rows // 2)
        waiting = state_refs[2][start : start + rows // 2]
    else:
        waiting = own_ref[rows:]
    return both, waiting.astype(jnp.float32)


def put_addends(last, refs, own, other, kept):
    tokens = own.shape[0]
    straight_ref, dtype = refs[0], refs[0].dtype
    straight_ref[:tokens] = own.astype(dtype)
    if last:
        refs[1][...] = other.astype(dtype)
        straight_ref[tokens:] = kept.astype(dtype)
        return
    straight_ref[tokens : 2 * tokens] = other.astype(dtype)
    if len(refs) == 2:
        straight_ref[2 * tokens :] = kept.astype(dtype)
        refs[1][:tokens] = own.astype(dtype)
        refs[1][tokens:] = other.astype(dtype)


def forward_kernel(fresh, last, counts, *refs):
    state_refs, (gain_ref,), weight_refs, (hidden_ref, slopes_ref, *addend_refs) = split(counts, refs)
    first, second = pair_state(fresh, 0, 0, state_refs)
    tokens, half = second.shape
    normed = (first * inverse_rms(first) * gain_ref[...]).astype(jnp.bfloat16)
    for span, weight_ref in spans(weight_refs):
        preact = lax.dot_general(
            normed,
            weight_ref[:, :half],
            (((1,), (1,)), ((), ())),
            preferred_element_type=jnp.float32,
        )
        normal_cdf = 0.5 * (1.0 + lax.erf(preact * root_half))
        density = jnp.exp(-0.5 * preact * preact) * inv_root_two_pi
        hidden_ref[:, span] = (preact * normal_cdf).astype(jnp.bfloat16)
        slopes_ref[:, span] = (normal_cdf + preact * density).astype(slopes_ref.dtype)
    branch = sum(
        jnp.dot(hidden_ref[:, span], weight_ref[:, half:], preferred_element_type=jnp.float32)
        for span, weight_ref in spans(weight_refs)
    )
    own = (second - branch[:tokens]) / coupling_scale
    other = (0.0 - branch[tokens:]) / coupling_scale
    put_addends(last, addend_refs, own, other, first[:tokens])


def backward_kernel(fresh, last, counts, *refs):
    acts_refs, state_refs, (gain_ref, slopes_ref), weight_refs, outs = split(counts, refs)
    cotangent_ref, *addend_refs, pre_grad = outs
    half = gain_ref.shape[1]
    second_grad, first_grad = pair_state(fresh, half, 1, state_refs)
    tokens = first_grad.shape[0]
    if not fresh:
        first_grad = coupling_scale * first_grad
    cotangent = second_grad.astype(jnp.bfloat16)
    cotangent_ref[...] = cotangent
    for span, weight_ref in spans(weight_refs):
        hidden_grad = lax.dot_general(
            cotangent,
            weight_ref[:, half:],
            (((1,), (1,)), ((), ())),
            preferred_element_type=jnp.float32,
        )
        slopes = slopes_ref[:, span].astype(jnp.float32)
        pre_grad[:, span] = (hidden_grad * slopes).astype(jnp.bfloat16)
    norm_grad = sum(
        jnp.dot(pre_grad[:, span], weight_ref[:, :half], preferred_element_type=jnp.float32)
        for span, weight_ref in spans(weight_refs)
    )
    first = pair_state(fresh, 0, None, acts_refs)[0]
    inv_rms = inverse_rms(first)
    scaled = norm_grad * gain_ref[...]
    inner = jnp.mean(first * scaled, axis=-1, keepdims=True)
    input_grad = inv_rms * scaled - first * (inv_rms * inv_rms * inv_rms) * inner
    own = first_grad + input_grad[:tokens]
    put_addends(last, addend_refs, own, input_grad[tokens:], cotangent[:tokens])


def cotangent_kernel(own_ref, other_ref, out_ref):
    rows = other_ref.shape[0]
    out_ref[...] = pair_sums(own_ref[:rows], other_ref[...]).astype(out_ref.dtype)


def output_kernel(kept_scale, kept_first, straight_ref, crossed_ref, out_ref):
    tokens, half = crossed_ref.shape
    fresh = straight_ref[:tokens].astype(jnp.float32) + crossed_ref[...].astype(jnp.float32)
    kept = straight_ref[tokens:].astype(jnp.float32)
    if kept_scale != 1.0:
        kept = kept * kept_scale
    first, second = (kept, fresh) if kept_first else (fresh, kept)
    out_ref[:, :half] = first
    out_ref[:, half:] = second


def outer_kernel(start, *refs):
    ticks = len(refs) // 2
    hidden_refs, cotangent_refs, out_ref = refs[:ticks], refs[ticks:-1], refs[-1]
    count = out_ref.shape[0]
    rows = jnp.concatenate([ref[:, start : start + count] for ref in hidden_refs], axis=0)
    cotangents = jnp.concatenate([ref[...] for ref in cotangent_refs], axis=0)
    total = lax.dot_general(
        rows, cotangents, (((0,), (0,)), ((), ())), preferred_element_type=jnp.float32
    )
    out_ref[...] = total.astype(out_ref.dtype)


def spans(weight_refs):
    offset = 0
    for ref in weight_refs:
        yield pl.ds(offset, ref.shape[0]), ref
        offset += ref.shape[0]


def in_vmem(count):
    return [pl.BlockSpec(memory_space=pltpu.VMEM)] * count


def cost(tokens, units, half):
    return pl.CostEstimate(
        flops=4 * tokens * units * half,
        bytes_accessed=4 * units * half + 4 * tokens * units,
        transcendentals=2 * tokens * units,
    )


def kernel_params():
    return pltpu.CompilerParams(vmem_limit_bytes=16 * 2**20)


def call(kernel, cost_estimate, outs, operands, scratch=()):
    return pl.pallas_call(
        kernel,
        out_shape=tuple(jax.ShapeDtypeStruct(shape, dtype) for shape, dtype in outs),
        in_specs=in_vmem(len(operands)),
        out_specs=tuple(in_vmem(len(outs))),
        scratch_shapes=list(scratch),
        cost_estimate=cost_estimate,
        compiler_params=kernel_params(),
    )(*operands)


def addend_shapes(fresh, last, tokens, half):
    if fresh:
        return (((2 * tokens, half), jnp.bfloat16),)
    straight, crossed = (2, 1) if last else (3, 2)
    return (
        ((straight * tokens, half), jnp.bfloat16),
        ((crossed * tokens, half), jnp.bfloat16),
    )


def forward(fresh, last, tokens, acts, gain, weights):
    half = gain.shape[1]
    units = sum(w.shape[0] for w in weights)
    return call(
        functools.partial(forward_kernel, fresh, last, (len(acts), 1, len(weights))),
        cost(2 * tokens, units, half),
        (
            ((2 * tokens, units), jnp.bfloat16),
            ((2 * tokens, units), jnp.bfloat16),
            *addend_shapes(fresh, last, tokens, half),
        ),
        (*acts, gain, *weights),
    )


def backward(fresh, last, tokens, acts, grads, gain, slopes, weights):
    half = gain.shape[1]
    units = slopes.shape[1]
    counts = (len(acts), len(grads), 2, len(weights))
    return call(
        functools.partial(backward_kernel, fresh, last, counts),
        cost(2 * tokens, units, half),
        (((2 * tokens, half), jnp.bfloat16), *addend_shapes(fresh, last, tokens, half)),
        (*acts, *grads, gain, slopes, *weights),
        (pltpu.VMEM((2 * tokens, units), jnp.bfloat16),),
    )


def small_cost(tokens, half):
    return pl.CostEstimate(
        flops=16 * tokens * half, bytes_accessed=16 * tokens * half, transcendentals=0
    )


def cotangent_of(grads):
    _, crossed = grads
    return call(
        cotangent_kernel, small_cost(*crossed.shape), ((crossed.shape, jnp.bfloat16),), grads
    )[0]


def output_of(kept_scale, kept_first, straight, crossed):
    tokens, half = crossed.shape
    return call(
        functools.partial(output_kernel, kept_scale, kept_first),
        small_cost(tokens, half),
        (((tokens, 2 * half), jnp.float32),),
        (straight, crossed),
    )[0]


def outer_rows(hiddens, cotangents, start, count):
    half = cotangents[0].shape[1]
    tokens = hiddens[0].shape[0] * len(hiddens)
    return call(
        functools.partial(outer_kernel, start),
        pl.CostEstimate(
            flops=2 * tokens * count * half,
            bytes_accessed=2 * (tokens * count + tokens * half + count * half),
            transcendentals=0,
        ),
        (((count, half), jnp.bfloat16),),
        (*hiddens, *cotangents),
    )[0]


def sent_back(straight, crossed=None):
    crossed = straight if crossed is None else crossed
    crossed = passed_back_to_partner(crossed)
    straight = passed_back(straight)
    return straight, crossed


def local(acts, grads, in_proj, out_proj, gain):
    tokens, half = acts.shape[1], acts.shape[2] // 2
    units = in_proj.shape[1]
    tick_count = min(4, lax.axis_size("section") // 2)
    shard = jnp.concatenate([in_proj[0], out_proj[0]], axis=1)
    group_size = len(alike_groups()[0])
    weights = gathered_along_x(exchanged(jnp.tile(shard, (group_size, 1))))
    quarter = group_size * units

    acts_pair = (acts[0], swapped_with_partner(acts[0, :, :half]))
    grads_pair = (grads[0], swapped_with_partner(grads[0, :, half:].astype(jnp.bfloat16)))
    sent_ahead = passed_back(
        jnp.concatenate([acts[0, :, :half], grads[0, :, half:]], axis=0).astype(jnp.bfloat16)
    )
    hiddens, cotangents = [], []
    for tick_index in range(tick_count):
        fresh, last = tick_index == 0, tick_index == tick_count - 1
        hidden, slopes, *addends = forward(fresh, last, tokens, acts_pair, gain, weights)
        hiddens.append(hidden)
        next_acts = sent_back(*addends)
        if last:
            grads_pair, hidden, addends = lax.optimization_barrier((grads_pair, hidden, addends))
            cotangents.append(cotangent_of(grads_pair))
            outer = functools.partial(outer_rows, hiddens, cotangents, count=quarter)
            far_rows = outer(3 * quarter)
            near_rows = outer(quarter)
            next_rows = outer(2 * quarter)
            from_far = swapped_along_x(far_rows, far_x)
            from_near = swapped_along_x(near_rows, near_x)
            from_next = swapped_along_x(next_rows, next_x)
            slopes, _ = lax.optimization_barrier((slopes, (far_rows, near_rows, next_rows)))
        cotangent, *addends = backward(
            fresh, last, tokens, acts_pair[:2], grads_pair, gain, slopes, weights
        )
        if last:
            own = outer(0)
            blocks = sum(
                x.astype(jnp.float32) for x in (own, from_near, from_next, from_far)
            ).astype(jnp.bfloat16)
            blocks, addends = lax.optimization_barrier((blocks, addends))
            parts = exchanged(blocks).reshape(-1, units, half)
        else:
            cotangents.append(cotangent)
        next_grads = sent_back(*addends)
        acts_pair, grads_pair = next_acts, next_grads
        if fresh:
            acts_pair, grads_pair = (*acts_pair, sent_ahead), (*grads_pair, sent_ahead)

    share = jnp.sum(parts.astype(jnp.float32), axis=0)
    acts_out = output_of(1.0, False, *acts_pair)
    grads_out = output_of(coupling_scale, True, *grads_pair)
    return (acts_out[None], grads_out[None], share[None])


def solution(mesh):
    pair = P("section", "dp", None)
    return jax.shard_map(
        local,
        mesh=mesh,
        in_specs=(pair, pair, pair, pair, P("section", None)),
        out_specs=(pair, pair, pair),
        check_vma=False,
    )
```

```python
import functools

import jax
import jax.numpy as jnp
from jax import lax
from jax.experimental import pallas as pl
from jax.experimental.pallas import tpu as pltpu
from jax.sharding import PartitionSpec as P


coupling_scale = 32.0**0.25
rms_epsilon = 1e-06
root_half = 0.7071067811865476
inv_root_two_pi = 0.3989422804014327

x_size = 4
pair_size = 2


def dp_index(z, x, y):
    return (z * x_size + x) * pair_size + y


def z_size():
    return lax.axis_size("dp") // (x_size * pair_size)


def alike_groups():
    return [
        [
            dp_index(z, x, y)
            for z in range(parity, z_size(), 2)
            for y in range(pair_size)
        ]
        for parity in range(2)
        for x in range(x_size)
    ]


def swapped_along_x(block, peer):
    route = [
        (dp_index(z, peer(x), y), dp_index(z, x, y))
        for z in range(z_size())
        for x in range(x_size)
        for y in range(pair_size)
    ]
    return lax.ppermute(block, "dp", route)


def partner(index):
    return index ^ (x_size * pair_size)


def swapped_with_partner(block):
    return lax.ppermute(block, "dp", [(partner(i), i) for i in range(lax.axis_size("dp"))])


def near_x(x):
    return x ^ 1


def next_x(x):
    return (x + 1 if x % 2 else x - 1) % x_size


def far_x(x):
    return (x + 2) % x_size


def exchanged(blocks):
    return lax.all_to_all(
        blocks, "dp", 0, 0, axis_index_groups=alike_groups(), tiled=True
    )


def passed_back(block):
    devices = range(lax.axis_size("section"))
    return lax.ppermute(block, "section", [(i, i - 1) for i in devices if i])


def passed_back_to_partner(block):
    size = lax.axis_size("dp")
    route = [
        (section * size + i, (section - 1) * size + partner(i))
        for section in range(1, lax.axis_size("section"))
        for i in range(size)
    ]
    return lax.ppermute(block, ("section", "dp"), route)


def gathered_along_x(block):
    rows = block.shape[0] // 2
    near, following = swapped_along_x(block, near_x), swapped_along_x(block, next_x)
    far_head = swapped_along_x(following[:rows], near_x)
    far_tail = swapped_along_x(near[rows:], next_x)
    return block, near, following, far_head, far_tail


def inverse_rms(first):
    return lax.rsqrt(jnp.mean(first * first, axis=-1, keepdims=True) + rms_epsilon)


def split(counts, refs):
    parts, start = [], 0
    for count in counts:
        parts.append(refs[start : start + count])
        start += count
    return *parts, refs[start:]


def pair_sums(straight, crossed):
    tokens = crossed.shape[0] // 2
    straight, crossed = straight.astype(jnp.float32), crossed.astype(jnp.float32)
    return jnp.concatenate(
        [straight[:tokens] + crossed[tokens:], straight[tokens:] + crossed[:tokens]], axis=0
    )


def pair_state(fresh, current, waiting_at, state_refs):
    own_ref, other_ref = state_refs[:2]
    if fresh:
        _, half = other_ref.shape
        waiting = half - current
        both = jnp.concatenate(
            [
                own_ref[:, current : current + half].astype(jnp.float32),
                other_ref[...].astype(jnp.float32),
            ],
            axis=0,
        )
        return both, own_ref[:, waiting : waiting + half]
    rows = other_ref.shape[0]
    both = pair_sums(own_ref[:rows], other_ref[...])
    if waiting_at is None:
        return both, None
    if len(state_refs) == 3:
        start = waiting_at * (rows // 2)
        waiting = state_refs[2][start : start + rows // 2]
    else:
        waiting = own_ref[rows:]
    return both, waiting.astype(jnp.float32)


def put_addends(last, refs, own, other, kept):
    tokens = own.shape[0]
    straight_ref, dtype = refs[0], refs[0].dtype
    straight_ref[:tokens] = own.astype(dtype)
    if last:
        refs[1][...] = other.astype(dtype)
        straight_ref[tokens:] = kept.astype(dtype)
        return
    straight_ref[tokens : 2 * tokens] = other.astype(dtype)
    if len(refs) == 2:
        straight_ref[2 * tokens :] = kept.astype(dtype)
        refs[1][:tokens] = own.astype(dtype)
        refs[1][tokens:] = other.astype(dtype)


def forward_kernel(fresh, last, counts, *refs):
    state_refs, (gain_ref,), weight_refs, (hidden_ref, slopes_ref, *addend_refs) = split(counts, refs)
    first, second = pair_state(fresh, 0, None if last else 0, state_refs)
    tokens, half = first.shape[0] // 2, first.shape[1]
    normed = (first * inverse_rms(first) * gain_ref[...]).astype(jnp.bfloat16)
    for span, weight_ref in spans(weight_refs):
        preact = lax.dot_general(
            normed,
            weight_ref[:, :half],
            (((1,), (1,)), ((), ())),
            preferred_element_type=jnp.float32,
        )
        normal_cdf = 0.5 * (1.0 + lax.erf(preact * root_half))
        density = jnp.exp(-0.5 * preact * preact) * inv_root_two_pi
        hidden_ref[:, span] = (preact * normal_cdf).astype(jnp.bfloat16)
        slopes_ref[:, span] = (normal_cdf + preact * density).astype(slopes_ref.dtype)
    branch = sum(
        jnp.dot(hidden_ref[:, span], weight_ref[:, half:], preferred_element_type=jnp.float32)
        for span, weight_ref in spans(weight_refs)
    )
    other = (0.0 - branch[tokens:]) / coupling_scale
    if last:
        crossed_ref, branch_ref, first_ref = addend_refs
        crossed_ref[...] = other.astype(crossed_ref.dtype)
        branch_ref[...] = branch[:tokens]
        first_ref[...] = first[:tokens].astype(first_ref.dtype)
        return
    own = (second - branch[:tokens]) / coupling_scale
    put_addends(last, addend_refs, own, other, first[:tokens])


def acts_end_kernel(waiting_ref, branch_ref, first_ref, out_ref):
    tokens = branch_ref.shape[0]
    second = waiting_ref[:tokens].astype(jnp.float32)
    out_ref[:tokens] = ((second - branch_ref[...]) / coupling_scale).astype(out_ref.dtype)
    out_ref[tokens:] = first_ref[...]


def backward_kernel(fresh, alone, last, counts, *refs):
    acts_refs, state_refs, (gain_ref, slopes_ref), weight_refs, outs = split(counts, refs)
    cotangent_ref, *addend_refs, pre_grad = outs
    ahead_ref = addend_refs.pop() if alone and not fresh else None
    half = gain_ref.shape[1]
    second_grad, first_grad = pair_state(fresh, half, 1, state_refs)
    tokens = first_grad.shape[0]
    if not fresh:
        first_grad = coupling_scale * first_grad
    cotangent = second_grad.astype(jnp.bfloat16)
    cotangent_ref[...] = cotangent
    for span, weight_ref in spans(weight_refs):
        hidden_grad = lax.dot_general(
            cotangent,
            weight_ref[:, half:],
            (((1,), (1,)), ((), ())),
            preferred_element_type=jnp.float32,
        )
        slopes = slopes_ref[:, span].astype(jnp.float32)
        pre_grad[:, span] = (hidden_grad * slopes).astype(jnp.bfloat16)
    norm_grad = sum(
        jnp.dot(pre_grad[:, span], weight_ref[:, :half], preferred_element_type=jnp.float32)
        for span, weight_ref in spans(weight_refs)
    )
    first = pair_state(fresh, 0, None, acts_refs)[0]
    if ahead_ref is not None:
        ahead_ref[:tokens] = first[:tokens].astype(ahead_ref.dtype)
        ahead_ref[tokens:] = cotangent[:tokens]
    inv_rms = inverse_rms(first)
    scaled = norm_grad * gain_ref[...]
    inner = jnp.mean(first * scaled, axis=-1, keepdims=True)
    input_grad = inv_rms * scaled - first * (inv_rms * inv_rms * inv_rms) * inner
    own = first_grad + input_grad[:tokens]
    put_addends(last, addend_refs, own, input_grad[tokens:], cotangent[:tokens])


def cotangent_kernel(own_ref, other_ref, out_ref):
    rows = other_ref.shape[0]
    out_ref[...] = pair_sums(own_ref[:rows], other_ref[...]).astype(out_ref.dtype)


def output_kernel(kept_scale, kept_first, straight_ref, crossed_ref, out_ref):
    tokens, half = crossed_ref.shape
    fresh = straight_ref[:tokens].astype(jnp.float32) + crossed_ref[...].astype(jnp.float32)
    kept = straight_ref[tokens:].astype(jnp.float32)
    if kept_scale != 1.0:
        kept = kept * kept_scale
    first, second = (kept, fresh) if kept_first else (fresh, kept)
    out_ref[:, :half] = first
    out_ref[:, half:] = second


def outer_kernel(start, *refs):
    ticks = len(refs) // 2
    hidden_refs, cotangent_refs, out_ref = refs[:ticks], refs[ticks:-1], refs[-1]
    count = out_ref.shape[0]
    rows = jnp.concatenate([ref[:, start : start + count] for ref in hidden_refs], axis=0)
    cotangents = jnp.concatenate([ref[...] for ref in cotangent_refs], axis=0)
    total = lax.dot_general(
        rows, cotangents, (((0,), (0,)), ((), ())), preferred_element_type=jnp.float32
    )
    out_ref[...] = total.astype(out_ref.dtype)


def spans(weight_refs):
    offset = 0
    for ref in weight_refs:
        yield pl.ds(offset, ref.shape[0]), ref
        offset += ref.shape[0]


def in_vmem(count):
    return [pl.BlockSpec(memory_space=pltpu.VMEM)] * count


def cost(tokens, units, half):
    return pl.CostEstimate(
        flops=4 * tokens * units * half,
        bytes_accessed=4 * units * half + 4 * tokens * units,
        transcendentals=2 * tokens * units,
    )


def kernel_params():
    return pltpu.CompilerParams(vmem_limit_bytes=16 * 2**20)


def call(kernel, cost_estimate, outs, operands, scratch=()):
    return pl.pallas_call(
        kernel,
        out_shape=tuple(jax.ShapeDtypeStruct(shape, dtype) for shape, dtype in outs),
        in_specs=in_vmem(len(operands)),
        out_specs=tuple(in_vmem(len(outs))),
        scratch_shapes=list(scratch),
        cost_estimate=cost_estimate,
        compiler_params=kernel_params(),
    )(*operands)


def addend_shapes(alone, last, tokens, half):
    if alone:
        return (((2 * tokens, half), jnp.bfloat16),)
    straight, crossed = (2, 1) if last else (3, 2)
    return (
        ((straight * tokens, half), jnp.bfloat16),
        ((crossed * tokens, half), jnp.bfloat16),
    )


def forward(fresh, alone, last, tokens, acts, gain, weights):
    half = gain.shape[1]
    addends = addend_shapes(alone, last, tokens, half)
    if last:
        block = (tokens, half)
        addends = ((block, jnp.bfloat16), (block, jnp.float32), (block, jnp.bfloat16))
    units = sum(w.shape[0] for w in weights)
    return call(
        functools.partial(forward_kernel, fresh, last, (len(acts), 1, len(weights))),
        cost(2 * tokens, units, half),
        (
            ((2 * tokens, units), jnp.bfloat16),
            ((2 * tokens, units), jnp.bfloat16),
            *addends,
        ),
        (*acts, gain, *weights),
    )


def acts_end(waiting, branch, first):
    tokens, half = branch.shape
    return call(
        acts_end_kernel,
        small_cost(tokens, half),
        (((2 * tokens, half), jnp.bfloat16),),
        (waiting, branch, first),
    )[0]


def backward(fresh, alone, last, tokens, acts, grads, gain, slopes, weights):
    half = gain.shape[1]
    ahead = (((2 * tokens, half), jnp.bfloat16),) if alone and not fresh else ()
    units = slopes.shape[1]
    counts = (len(acts), len(grads), 2, len(weights))
    return call(
        functools.partial(backward_kernel, fresh, alone, last, counts),
        cost(2 * tokens, units, half),
        (((2 * tokens, half), jnp.bfloat16), *addend_shapes(alone, last, tokens, half), *ahead),
        (*acts, *grads, gain, slopes, *weights),
        (pltpu.VMEM((2 * tokens, units), jnp.bfloat16),),
    )


def small_cost(tokens, half):
    return pl.CostEstimate(
        flops=16 * tokens * half, bytes_accessed=16 * tokens * half, transcendentals=0
    )


def cotangent_of(grads):
    _, crossed = grads
    return call(
        cotangent_kernel, small_cost(*crossed.shape), ((crossed.shape, jnp.bfloat16),), grads
    )[0]


def output_of(kept_scale, kept_first, straight, crossed):
    tokens, half = crossed.shape
    return call(
        functools.partial(output_kernel, kept_scale, kept_first),
        small_cost(tokens, half),
        (((tokens, 2 * half), jnp.float32),),
        (straight, crossed),
    )[0]


def outer_rows(hiddens, cotangents, start, count):
    half = cotangents[0].shape[1]
    tokens = hiddens[0].shape[0] * len(hiddens)
    return call(
        functools.partial(outer_kernel, start),
        pl.CostEstimate(
            flops=2 * tokens * count * half,
            bytes_accessed=2 * (tokens * count + tokens * half + count * half),
            transcendentals=0,
        ),
        (((count, half), jnp.bfloat16),),
        (*hiddens, *cotangents),
    )[0]


def sent_back(straight, crossed=None):
    crossed = straight if crossed is None else crossed
    crossed = passed_back_to_partner(crossed)
    straight = passed_back(straight)
    return straight, crossed


def local(acts, grads, in_proj, out_proj, gain):
    tokens, half = acts.shape[1], acts.shape[2] // 2
    units = in_proj.shape[1]
    tick_count = min(4, lax.axis_size("section") // 2)
    shard = jnp.concatenate([in_proj[0], out_proj[0]], axis=1)
    group_size = len(alike_groups()[0])
    weights = gathered_along_x(exchanged(jnp.tile(shard, (group_size, 1))))
    quarter = group_size * units

    acts_pair = (acts[0], swapped_with_partner(acts[0, :, :half]))
    grads_pair = (grads[0], swapped_with_partner(grads[0, :, half:].astype(jnp.bfloat16)))
    sent_ahead = passed_back(
        jnp.concatenate([acts[0, :, :half], grads[0, :, half:]], axis=0).astype(jnp.bfloat16)
    )
    hiddens, cotangents = [], []
    for tick_index in range(tick_count):
        fresh, last = tick_index == 0, tick_index == tick_count - 1
        alone = tick_index in (0, tick_count - 2)
        state = acts_pair[:2] if last else acts_pair
        hidden, slopes, *addends = forward(fresh, alone, last, tokens, state, gain, weights)
        hiddens.append(hidden)
        if last:
            crossed, branch, first = addends
            crossed = passed_back_to_partner(crossed)
            straight = passed_back(acts_end(acts_pair[2], branch, first))
            next_acts = straight, crossed
        else:
            next_acts = sent_back(*addends)
        if last:
            straight, crossed, hidden = lax.optimization_barrier((*grads_pair[:2], hidden))
            grads_pair = (straight, crossed, grads_pair[2])
            cotangents.append(cotangent_of(grads_pair[:2]))
            outer = functools.partial(outer_rows, hiddens, cotangents, count=quarter)
            far_rows = outer(3 * quarter)
            near_rows = outer(quarter)
            next_rows = outer(2 * quarter)
            from_far = swapped_along_x(far_rows, far_x)
            from_near = swapped_along_x(near_rows, near_x)
            from_next = swapped_along_x(next_rows, next_x)
            slopes, _ = lax.optimization_barrier((slopes, (far_rows, near_rows, next_rows)))
        cotangent, *addends = backward(
            fresh, alone, last, tokens, acts_pair[:2], grads_pair, gain, slopes, weights
        )
        if last:
            own = outer(0)
            blocks = sum(
                x.astype(jnp.float32) for x in (own, from_near, from_next, from_far)
            ).astype(jnp.bfloat16)
            blocks, addends = lax.optimization_barrier((blocks, addends))
            parts = exchanged(blocks).reshape(-1, units, half)
        else:
            cotangents.append(cotangent)
        ahead = addends.pop() if alone and not fresh else None
        next_grads = sent_back(*addends)
        if ahead is not None:
            sent_ahead = passed_back(ahead)
        acts_pair, grads_pair = next_acts, next_grads
        if alone:
            acts_pair, grads_pair = (*acts_pair, sent_ahead), (*grads_pair, sent_ahead)

    share = jnp.sum(parts.astype(jnp.float32), axis=0)
    acts_out = output_of(1.0, False, *acts_pair)
    grads_out = output_of(coupling_scale, True, *grads_pair)
    return (acts_out[None], grads_out[None], share[None])


def solution(mesh):
    pair = P("section", "dp", None)
    return jax.shard_map(
        local,
        mesh=mesh,
        in_specs=(pair, pair, pair, pair, P("section", None)),
        out_specs=(pair, pair, pair),
        check_vma=False,
    )
```

```python
import functools

import jax
import jax.numpy as jnp
from jax import lax
from jax.experimental import pallas as pl
from jax.experimental.pallas import tpu as pltpu
from jax.sharding import PartitionSpec as P


coupling_scale = 32.0**0.25
rms_epsilon = 1e-06
root_half = 0.7071067811865476
inv_root_two_pi = 0.3989422804014327

x_size = 4
pair_size = 2


def dp_index(z, x, y):
    return (z * x_size + x) * pair_size + y


def z_size():
    return lax.axis_size("dp") // (x_size * pair_size)


def alike_groups():
    return [
        [
            dp_index(z, x, y)
            for z in range(parity, z_size(), 2)
            for y in range(pair_size)
        ]
        for parity in range(2)
        for x in range(x_size)
    ]


def swapped_along_x(block, peer):
    route = [
        (dp_index(z, peer(x), y), dp_index(z, x, y))
        for z in range(z_size())
        for x in range(x_size)
        for y in range(pair_size)
    ]
    return lax.ppermute(block, "dp", route)


def partner(index):
    return index ^ (x_size * pair_size)


def swapped_with_partner(block):
    return lax.ppermute(block, "dp", [(partner(i), i) for i in range(lax.axis_size("dp"))])


def near_x(x):
    return x ^ 1


def next_x(x):
    return (x + 1 if x % 2 else x - 1) % x_size


def far_x(x):
    return (x + 2) % x_size


def exchanged(blocks):
    return lax.all_to_all(
        blocks, "dp", 0, 0, axis_index_groups=alike_groups(), tiled=True
    )


def passed_back(block):
    devices = range(lax.axis_size("section"))
    return lax.ppermute(block, "section", [(i, i - 1) for i in devices if i])


def passed_back_to_partner(block):
    size = lax.axis_size("dp")
    route = [
        (section * size + i, (section - 1) * size + partner(i))
        for section in range(1, lax.axis_size("section"))
        for i in range(size)
    ]
    return lax.ppermute(block, ("section", "dp"), route)


def gathered_along_x(block):
    rows = block.shape[0] // 2
    near, following = swapped_along_x(block, near_x), swapped_along_x(block, next_x)
    far_head = swapped_along_x(following[:rows], near_x)
    far_tail = swapped_along_x(near[rows:], next_x)
    return block, near, following, far_head, far_tail


def inverse_rms(first):
    return lax.rsqrt(jnp.mean(first * first, axis=-1, keepdims=True) + rms_epsilon)


def split(counts, refs):
    parts, start = [], 0
    for count in counts:
        parts.append(refs[start : start + count])
        start += count
    return *parts, refs[start:]


def pair_sums(straight, crossed):
    tokens = crossed.shape[0] // 2
    straight, crossed = straight.astype(jnp.float32), crossed.astype(jnp.float32)
    return jnp.concatenate(
        [straight[:tokens] + crossed[tokens:], straight[tokens:] + crossed[:tokens]], axis=0
    )


def pair_state(fresh, current, waiting_at, state_refs):
    own_ref, other_ref = state_refs[:2]
    if fresh:
        _, half = other_ref.shape
        waiting = half - current
        both = jnp.concatenate(
            [
                own_ref[:, current : current + half].astype(jnp.float32),
                other_ref[...].astype(jnp.float32),
            ],
            axis=0,
        )
        return both, own_ref[:, waiting : waiting + half]
    rows = other_ref.shape[0]
    both = pair_sums(own_ref[:rows], other_ref[...])
    if waiting_at is None:
        return both, None
    if len(state_refs) == 3:
        start = waiting_at * (rows // 2)
        waiting = state_refs[2][start : start + rows // 2]
    else:
        waiting = own_ref[rows:]
    return both, waiting.astype(jnp.float32)


def put_addends(last, refs, own, other, kept):
    tokens = own.shape[0]
    straight_ref, dtype = refs[0], refs[0].dtype
    straight_ref[:tokens] = own.astype(dtype)
    if last:
        refs[1][...] = other.astype(dtype)
        straight_ref[tokens:] = kept.astype(dtype)
        return
    straight_ref[tokens : 2 * tokens] = other.astype(dtype)
    if len(refs) == 2:
        straight_ref[2 * tokens :] = kept.astype(dtype)
        refs[1][:tokens] = own.astype(dtype)
        refs[1][tokens:] = other.astype(dtype)


def forward_kernel(fresh, last, counts, *refs):
    state_refs, (gain_ref,), weight_refs, (hidden_ref, slopes_ref, *addend_refs) = split(counts, refs)
    first, second = pair_state(fresh, 0, 0, state_refs)
    tokens, half = second.shape
    normed = (first * inverse_rms(first) * gain_ref[...]).astype(jnp.bfloat16)
    for span, weight_ref in spans(weight_refs):
        preact = lax.dot_general(
            normed,
            weight_ref[:, :half],
            (((1,), (1,)), ((), ())),
            preferred_element_type=jnp.float32,
        )
        normal_cdf = 0.5 * (1.0 + lax.erf(preact * root_half))
        density = jnp.exp(-0.5 * preact * preact) * inv_root_two_pi
        hidden_ref[:, span] = (preact * normal_cdf).astype(jnp.bfloat16)
        slopes_ref[:, span] = (normal_cdf + preact * density).astype(slopes_ref.dtype)
    branch = sum(
        jnp.dot(hidden_ref[:, span], weight_ref[:, half:], preferred_element_type=jnp.float32)
        for span, weight_ref in spans(weight_refs)
    )
    own = (second - branch[:tokens]) / coupling_scale
    other = (0.0 - branch[tokens:]) / coupling_scale
    put_addends(last, addend_refs, own, other, first[:tokens])


def backward_kernel(fresh, last, counts, *refs):
    acts_refs, state_refs, (gain_ref, slopes_ref), weight_refs, outs = split(counts, refs)
    cotangent_ref, *addend_refs, pre_grad = outs
    half = gain_ref.shape[1]
    second_grad, first_grad = pair_state(fresh, half, 1, state_refs)
    tokens = first_grad.shape[0]
    if not fresh:
        first_grad = coupling_scale * first_grad
    cotangent = second_grad.astype(jnp.bfloat16)
    cotangent_ref[...] = cotangent
    for span, weight_ref in spans(weight_refs):
        hidden_grad = lax.dot_general(
            cotangent,
            weight_ref[:, half:],
            (((1,), (1,)), ((), ())),
            preferred_element_type=jnp.float32,
        )
        slopes = slopes_ref[:, span].astype(jnp.float32)
        pre_grad[:, span] = (hidden_grad * slopes).astype(jnp.bfloat16)
    norm_grad = sum(
        jnp.dot(pre_grad[:, span], weight_ref[:, :half], preferred_element_type=jnp.float32)
        for span, weight_ref in spans(weight_refs)
    )
    first = pair_state(fresh, 0, None, acts_refs)[0]
    inv_rms = inverse_rms(first)
    scaled = norm_grad * gain_ref[...]
    inner = jnp.mean(first * scaled, axis=-1, keepdims=True)
    input_grad = inv_rms * scaled - first * (inv_rms * inv_rms * inv_rms) * inner
    own = first_grad + input_grad[:tokens]
    put_addends(last, addend_refs, own, input_grad[tokens:], cotangent[:tokens])


def cotangent_kernel(own_ref, other_ref, out_ref):
    rows = other_ref.shape[0]
    out_ref[...] = pair_sums(own_ref[:rows], other_ref[...]).astype(out_ref.dtype)


def output_kernel(kept_scale, kept_first, straight_ref, crossed_ref, out_ref):
    tokens, half = crossed_ref.shape
    fresh = straight_ref[:tokens].astype(jnp.float32) + crossed_ref[...].astype(jnp.float32)
    kept = straight_ref[tokens:].astype(jnp.float32)
    if kept_scale != 1.0:
        kept = kept * kept_scale
    first, second = (kept, fresh) if kept_first else (fresh, kept)
    out_ref[:, :half] = first
    out_ref[:, half:] = second


def outer_kernel(start, *refs):
    ticks = len(refs) // 2
    hidden_refs, cotangent_refs, out_ref = refs[:ticks], refs[ticks:-1], refs[-1]
    count = out_ref.shape[0]
    rows = jnp.concatenate([ref[:, start : start + count] for ref in hidden_refs], axis=0)
    cotangents = jnp.concatenate([ref[...] for ref in cotangent_refs], axis=0)
    total = lax.dot_general(
        rows, cotangents, (((0,), (0,)), ((), ())), preferred_element_type=jnp.float32
    )
    out_ref[...] = total.astype(out_ref.dtype)


def spans(weight_refs):
    offset = 0
    for ref in weight_refs:
        yield pl.ds(offset, ref.shape[0]), ref
        offset += ref.shape[0]


def in_vmem(count):
    return [pl.BlockSpec(memory_space=pltpu.VMEM)] * count


def cost(tokens, units, half):
    return pl.CostEstimate(
        flops=4 * tokens * units * half,
        bytes_accessed=4 * units * half + 4 * tokens * units,
        transcendentals=2 * tokens * units,
    )


def kernel_params():
    return pltpu.CompilerParams(vmem_limit_bytes=16 * 2**20)


def call(kernel, cost_estimate, outs, operands, scratch=()):
    return pl.pallas_call(
        kernel,
        out_shape=tuple(jax.ShapeDtypeStruct(shape, dtype) for shape, dtype in outs),
        in_specs=in_vmem(len(operands)),
        out_specs=tuple(in_vmem(len(outs))),
        scratch_shapes=list(scratch),
        cost_estimate=cost_estimate,
        compiler_params=kernel_params(),
    )(*operands)


def addend_shapes(fresh, last, tokens, half):
    if fresh:
        return (((2 * tokens, half), jnp.bfloat16),)
    straight, crossed = (2, 1) if last else (3, 2)
    return (
        ((straight * tokens, half), jnp.bfloat16),
        ((crossed * tokens, half), jnp.bfloat16),
    )


def forward(fresh, last, tokens, acts, gain, weights):
    half = gain.shape[1]
    units = sum(w.shape[0] for w in weights)
    return call(
        functools.partial(forward_kernel, fresh, last, (len(acts), 1, len(weights))),
        cost(2 * tokens, units, half),
        (
            ((2 * tokens, units), jnp.bfloat16),
            ((2 * tokens, units), jnp.bfloat16),
            *addend_shapes(fresh, last, tokens, half),
        ),
        (*acts, gain, *weights),
    )


def backward(fresh, last, tokens, acts, grads, gain, slopes, weights):
    half = gain.shape[1]
    units = slopes.shape[1]
    counts = (len(acts), len(grads), 2, len(weights))
    return call(
        functools.partial(backward_kernel, fresh, last, counts),
        cost(2 * tokens, units, half),
        (((2 * tokens, half), jnp.bfloat16), *addend_shapes(fresh, last, tokens, half)),
        (*acts, *grads, gain, slopes, *weights),
        (pltpu.VMEM((2 * tokens, units), jnp.bfloat16),),
    )


def small_cost(tokens, half):
    return pl.CostEstimate(
        flops=16 * tokens * half, bytes_accessed=16 * tokens * half, transcendentals=0
    )


def cotangent_of(grads):
    _, crossed = grads
    return call(
        cotangent_kernel, small_cost(*crossed.shape), ((crossed.shape, jnp.bfloat16),), grads
    )[0]


def output_of(kept_scale, kept_first, straight, crossed):
    tokens, half = crossed.shape
    return call(
        functools.partial(output_kernel, kept_scale, kept_first),
        small_cost(tokens, half),
        (((tokens, 2 * half), jnp.float32),),
        (straight, crossed),
    )[0]


def outer_rows(hiddens, cotangents, start, count):
    half = cotangents[0].shape[1]
    tokens = hiddens[0].shape[0] * len(hiddens)
    return call(
        functools.partial(outer_kernel, start),
        pl.CostEstimate(
            flops=2 * tokens * count * half,
            bytes_accessed=2 * (tokens * count + tokens * half + count * half),
            transcendentals=0,
        ),
        (((count, half), jnp.bfloat16),),
        (*hiddens, *cotangents),
    )[0]


def sum_kernel(*refs):
    total = sum(ref[...].astype(jnp.float32) for ref in refs[:-1])
    refs[-1][...] = total.astype(refs[-1].dtype)


def sum_of(*parts):
    shape = parts[0].shape
    return call(sum_kernel, small_cost(*shape), ((shape, jnp.bfloat16),), parts)[0]


def sent_back(straight, crossed=None):
    crossed = straight if crossed is None else crossed
    crossed = passed_back_to_partner(crossed)
    straight = passed_back(straight)
    return straight, crossed


def local(acts, grads, in_proj, out_proj, gain):
    tokens, half = acts.shape[1], acts.shape[2] // 2
    units = in_proj.shape[1]
    tick_count = min(4, lax.axis_size("section") // 2)
    shard = jnp.concatenate([in_proj[0], out_proj[0]], axis=1)
    group_size = len(alike_groups()[0])
    weights = gathered_along_x(exchanged(jnp.tile(shard, (group_size, 1))))
    quarter = group_size * units

    acts_pair = (acts[0], swapped_with_partner(acts[0, :, :half]))
    grads_pair = (grads[0], swapped_with_partner(grads[0, :, half:].astype(jnp.bfloat16)))
    sent_ahead = passed_back(
        jnp.concatenate([acts[0, :, :half], grads[0, :, half:]], axis=0).astype(jnp.bfloat16)
    )
    hiddens, cotangents = [], []
    for tick_index in range(tick_count):
        fresh, last = tick_index == 0, tick_index == tick_count - 1
        hidden, slopes, *addends = forward(fresh, last, tokens, acts_pair, gain, weights)
        hiddens.append(hidden)
        next_acts = sent_back(*addends)
        if last:
            grads_pair, hidden, addends = lax.optimization_barrier((grads_pair, hidden, addends))
            cotangents.append(cotangent_of(grads_pair))
            outer = functools.partial(outer_rows, hiddens, cotangents, count=quarter)
            far_rows = outer(3 * quarter)
            near_rows = outer(quarter)
            next_rows = outer(2 * quarter)
            from_far = swapped_along_x(far_rows, far_x)
            from_near = swapped_along_x(near_rows, near_x)
            from_next = swapped_along_x(next_rows, next_x)
            slopes, _ = lax.optimization_barrier((slopes, (far_rows, near_rows, next_rows)))
        cotangent, *addends = backward(
            fresh, last, tokens, acts_pair[:2], grads_pair, gain, slopes, weights
        )
        if last:
            own = outer(0)
            blocks = sum_of(own, from_near, from_next, from_far)
            blocks, addends = lax.optimization_barrier((blocks, addends))
            parts = exchanged(blocks).reshape(-1, units, half)
        else:
            cotangents.append(cotangent)
        next_grads = sent_back(*addends)
        acts_pair, grads_pair = next_acts, next_grads
        if fresh:
            acts_pair, grads_pair = (*acts_pair, sent_ahead), (*grads_pair, sent_ahead)

    share = jnp.sum(parts.astype(jnp.float32), axis=0)
    acts_out = output_of(1.0, False, *acts_pair)
    grads_out = output_of(coupling_scale, True, *grads_pair)
    return (acts_out[None], grads_out[None], share[None])


def solution(mesh):
    pair = P("section", "dp", None)
    return jax.shard_map(
        local,
        mesh=mesh,
        in_specs=(pair, pair, pair, pair, P("section", None)),
        out_specs=(pair, pair, pair),
        check_vma=False,
    )
```
